128 devices in a mesh: grp: 2 (over x_hi), row: 8 (over x_lo, z), col: 8 (over y, core).
Axes of the slice: x: 4 (x_hi: 2, x_lo: 2; x = x_hi * 2 + x_lo), y: 4, z: 4, core: 2. Of those that a mesh axis runs over, the one named last changes fastest.
Arguments:
- activations: bfloat16 [256, 64, 8192], P(('grp', 'col'), None, 'row'), may hold values from -6 to 6
- out_grads: bfloat16 [256, 64, 8192], P(('grp', 'col'), None, 'row'), may hold values from -6 to 6
- proj_in: bfloat16 [8192, 128], P('row'), may hold values from -0.0625 to 0.0625
- proj_out: bfloat16 [8192, 128], P('row'), may hold values from -0.0625 to 0.0625
- fisher_inv: float32 [16384, 16384], P('row', ('grp', 'col')), may hold values from -1 to 4, as said below
- store: bfloat16 [32768, 16384], P('row', ('grp', 'col')), may hold values from -0.046875 to 0.046875
- lengths: int32 [256], P(('grp', 'col')), may hold values from 1 to 64, as said below
- judge_ids: int32 [256], replicated, may hold values from 0 to 127, as said below
Outputs:
- node_scores: float32 [32768, 128], P('row')
The draws below stay inside these ranges and needn't reach their ends.
Inputs may be any that keep to these rules, and one draw needn't show every extreme that they name: lengths[b] is how many of branch b's first token slots count; the rest are padding. `judge_ids`: every node id names at least one branch. fisher_inv is symmetric.
All inputs are finite; a program needn't handle non-finite values.
Results may differ from the reference program's by a relative error of at most 0.0029.
Values may be sent and summed in bfloat16 or wider, within the bound.
A program may use at most 128 MiB of HBM per device.

```python
import math
import jax
import jax.numpy as jnp
from jax import lax

D = 8192
RANK = 128
L = 64
FEATS = 16384
BRANCHES = 256
STORE = 32768
NODES = 128


def draw_fisher_inv(key, part):
    key_off = jax.random.fold_in(key, 11)
    key_diag = jax.random.fold_in(key, 12)
    spread = 0.5
    diag_vals = jnp.exp(jax.random.uniform(key_diag, (FEATS,), jnp.float32, jnp.log(0.5), jnp.log(2.0)))
    base = jnp.clip(jax.random.normal(key_off, (FEATS, FEATS), jnp.float32), -6.0, 6.0) * (spread / jnp.sqrt(FEATS * 1.0))
    symmetric = base + base.T
    return symmetric + jnp.diag(diag_vals)


def draw_lengths(key, part):
    key_len = jax.random.fold_in(key, 21)
    key_pick = jax.random.fold_in(key, 22)
    drawn = jax.random.randint(key_len, (BRANCHES,), 1, L + 1)
    picked = jax.random.randint(key_pick, (), 0, BRANCHES)
    return jnp.where(jnp.arange(BRANCHES) == picked, L, drawn).astype(jnp.int32)


def draw_judge_ids(key, part):
    key_first = jax.random.fold_in(key, 31)
    key_rest = jax.random.fold_in(key, 32)
    key_order = jax.random.fold_in(key, 33)
    first = jax.random.permutation(key_first, NODES)
    rest = jax.random.randint(key_rest, (BRANCHES - NODES,), 0, NODES)
    joined = jnp.concatenate([first.astype(jnp.int32), rest.astype(jnp.int32)])
    return jax.random.permutation(key_order, joined).astype(jnp.int32)


def shard_levels(key, shape, cuts, smallest, largest):
    level = 1.0
    for position, blocks in cuts:
        steps = jax.random.uniform(jax.random.fold_in(jax.random.fold_in(key, 6), position), (blocks,), jnp.float32, smallest / len(cuts), largest / len(cuts))
        level = level * jnp.repeat(jnp.exp(steps), shape[position] // blocks).reshape((-1,) + (1,) * (len(shape) - 1 - position))
    return level


def gaussian(stream_key, shape, deviation, reach, cuts=(), held_as=jnp.bfloat16):
    array = jax.random.normal(stream_key, shape, jnp.float32) * deviation
    if len(cuts) > 0:
        array = shard_levels(stream_key, shape, cuts, -0.22, 0.18) * array
    return jnp.clip(array, min=-reach, max=reach).astype(held_as)


def setup_inputs(seed: int = 0) -> dict:
    keys = jax.random.split(jax.random.key(seed), 9)
    activations = gaussian(keys[0], (BRANCHES, L, D), 1.0, 6.0, ((0, 16), (2, 8)))
    out_grads = gaussian(keys[1], (BRANCHES, L, D), 1.0, 6.0, ((0, 16), (2, 8)))
    proj_in = gaussian(keys[2], (D, RANK), D ** -0.5, 0.0625, ((0, 8),))
    proj_out = gaussian(keys[3], (D, RANK), D ** -0.5, 0.0625, ((0, 8),))
    fisher_inv = draw_fisher_inv(jax.random.fold_in(keys[8], 71), 0)
    store = gaussian(keys[5], (STORE, FEATS), FEATS ** -0.5, 0.046875, ((0, 8), (1, 16)))
    lengths = draw_lengths(jax.random.fold_in(keys[8], 71), 0)
    judge_ids = draw_judge_ids(jax.random.fold_in(keys[8], 71), 0)
    return {"activations": activations, "out_grads": out_grads, "proj_in": proj_in, "proj_out": proj_out, "fisher_inv": fisher_inv, "store": store, "lengths": lengths, "judge_ids": judge_ids}


def reference(activations, out_grads, proj_in, proj_out, fisher_inv, store, lengths, judge_ids):
    high = lax.Precision.HIGHEST
    flat_act = activations.reshape(BRANCHES * L, D).astype(jnp.float32)
    flat_grad = out_grads.reshape(BRANCHES * L, D).astype(jnp.float32)
    act_proj = jnp.dot(flat_act, proj_in.astype(jnp.float32), precision=high).reshape(BRANCHES, L, RANK)
    grad_proj = jnp.dot(flat_grad, proj_out.astype(jnp.float32), precision=high).reshape(BRANCHES, L, RANK)
    token_mask = (jnp.arange(L)[None, :] < lengths[:, None]).astype(jnp.float32)
    weighted = grad_proj * token_mask[:, :, None]
    grads = jnp.einsum('bto,bti->boi', weighted, act_proj, precision=high) * (1.0 / math.sqrt(L))
    grads = grads.reshape(BRANCHES, FEATS)
    pre = lax.dot_general(fisher_inv, grads, (((1,), (1,)), ((), ())), precision=high)
    pre_half = pre.astype(jnp.bfloat16)
    scores = jnp.dot(store.astype(jnp.float32), pre_half.astype(jnp.float32), precision=high)
    onehot = (judge_ids[:, None] == jnp.arange(NODES)[None, :]).astype(jnp.float32)
    return jnp.dot(scores, onehot, precision=high)
```

```python
import functools
import math

import jax
import jax.numpy as jnp
from jax import lax
from jax.experimental import pallas as pl
from jax.experimental.pallas import tpu as pltpu
from jax.sharding import PartitionSpec as P

MESH = pl.DeviceIdType.MESH
F32 = jnp.float32
BF16 = jnp.bfloat16
SPAN = 80.0
MROWS = 16


def bound(x):
    top = jnp.max(jnp.abs(x), axis=0, keepdims=True)
    return (top * 1.01 + 1e-36).astype(BF16)


def encode(x, m):
    y = jnp.exp(jnp.abs(x) * (SPAN / m) - 0.5 * SPAN)
    return jnp.where(x < 0, -y, y).astype(BF16)


def decode(y, m):
    y = y.astype(F32)
    t = (jnp.log(jnp.abs(y)) + 0.5 * SPAN) * (m / SPAN)
    return jnp.where(y < 0, -t, t)


def pack(ref, start, x, mstart, mrows=MROWS):
    m = bound(x)
    rows = x.shape[0]
    ref[start:start + rows, :] = encode(x, m.astype(F32))
    ref[mstart:mstart + mrows, :] = jnp.broadcast_to(m, (mrows, x.shape[1]))


def unpack(ref, start, rows, mstart):
    return decode(ref[start:start + rows, :], ref[mstart:mstart + 16, :][:1].astype(F32))


def split(x):
    hi = x.astype(BF16)
    return hi, (x - hi.astype(F32)).astype(BF16)


def dot(a, b):
    return jnp.dot(a, b, preferred_element_type=F32)


def kernel(
    act, og, pin, pout, fish, store, lens, ids, out,
    actv, ogv, pinv, poutv, fv, fhi, flo, sv,
    p1s, p1r, acc_a, acc_g, p2s, p2r, p3, gf, amat,
    p4s, p4r, acc4, p5, p6s, p6r, p7s, p7r, acc7, ob,
    ld1, ldw, ldf, lds, ldo,
    p1ss, p1rs, p2ss, p2rs, p3ss, p3rs, f3ss, f3rs, p4ss, p4rs, p5ss, p5rs,
    p6ss, p6rs, p7ss, p7rs, p8ss, p8rs, f8ss, f8rs,
):
    g = lax.axis_index("grp")
    r = lax.axis_index("row")
    col = lax.axis_index("col")
    y, core = col // 2, col % 2
    q = g * 4 + y
    c = q * 2 + core
    sib = col + 1 - 2 * core

    def ahead(i, k):
        return ((i // 4 + k // 4) % 2) * 4 + (i % 4 + k % 4) % 4

    def behind(i, k):
        return ((i // 4 + k // 4) % 2) * 4 + (i % 4 + 4 - k % 4) % 4

    def to_row(i):
        return {"row": i}

    def to_chip(i):
        return {"grp": i // 4, "col": (i % 4) * 2 + core}

    to_sib = {"col": sib}

    def remote(src, dst, ss, rs, dev):
        return pltpu.make_async_remote_copy(
            src_ref=src, dst_ref=dst, send_sem=ss, recv_sem=rs, device_id=dev, device_id_type=MESH)

    pltpu.make_async_copy(pin, pinv, ldw.at[0]).start()
    pltpu.make_async_copy(pout, poutv, ldw.at[1]).start()

    def tokens(k):
        rows = pl.ds(pl.multiple_of(ahead(r, k % 8) * 128, 128), 128)
        return (pltpu.make_async_copy(act.at[rows, :], actv.at[rows, :], ld1.at[0, k]),
                pltpu.make_async_copy(og.at[rows, :], ogv.at[rows, :], ld1.at[1, k]))

    def start_tokens(k, _):
        for cp in tokens(k):
            cp.start()
        return 0
    lax.fori_loop(1, 9, start_tokens, 0)

    barrier = pltpu.get_barrier_semaphore()

    def greet(k, _):
        pl.semaphore_signal(barrier, inc=1, device_id=to_row(ahead(r, k)), device_id_type=MESH)
        pl.semaphore_signal(barrier, inc=1, device_id=to_chip(ahead(q, k)), device_id_type=MESH)
        return 0
    lax.fori_loop(1, 8, greet, 0)
    pl.semaphore_signal(barrier, inc=1, device_id=to_sib, device_id_type=MESH)
    pl.semaphore_wait(barrier, 15)

    def project(k):
        rows = pl.ds(pl.multiple_of(ahead(r, k % 8) * 128, 128), 128)
        for cp in tokens(k):
            cp.wait()
        return dot(actv[rows, :], pinv[...]), dot(ogv[rows, :], poutv[...])

    pltpu.make_async_copy(pin, pinv, ldw.at[0]).wait()
    pltpu.make_async_copy(pout, poutv, ldw.at[1]).wait()

    def p1_copy(k):
        return remote(p1s.at[k], p1r.at[k], p1ss.at[k], p1rs.at[k], to_row(ahead(r, k)))

    def p1_send(k, _):
        a, b = project(k)
        buf = p1s.at[k]
        pack(buf, 0, a, 256)
        pack(buf, 128, b, 272)
        p1_copy(k).start()
        return 0
    lax.fori_loop(1, 8, p1_send, 0)
    a, b = project(8)
    acc_a[...] = a
    acc_g[...] = b

    def f_load(i):
        rows = pl.ds(pl.multiple_of(i * 256, 256), 256)
        return pltpu.make_async_copy(fish.at[rows, :], fv.at[rows, :], ldf.at[i])

    def f_start(i, _):
        f_load(i).start()
        return 0
    lax.fori_loop(0, 8, f_start, 0)

    def f_split(i, _):
        f_load(i).wait()

        def part(j, _):
            rows = pl.ds(pl.multiple_of(i * 256 + j * 32, 32), 32)
            hi, lo = split(fv[rows, :])
            fhi[rows, :] = hi
            flo[rows, :] = lo
            return 0
        lax.fori_loop(0, 8, part, 0)
        return 0
    lax.fori_loop(0, 8, f_split, 0)
    store_copy = pltpu.make_async_copy(store, sv, lds)
    store_copy.start()

    def p1_recv(k, _):
        p1_copy(k).wait_recv()
        buf = p1r.at[k]
        acc_a[...] += unpack(buf, 0, 128, 256)
        acc_g[...] += unpack(buf, 128, 128, 272)
        return 0
    lax.fori_loop(1, 8, p1_recv, 0)

    place = lax.broadcasted_iota(jnp.int32, (128, 128), 0)
    limit = jnp.where(place < 64, lens[2 * r], lens[2 * r + 1] + 64)
    weighted = jnp.where(place < limit, acc_g[...], 0.0)
    for j in range(2):
        p2s[j] = lax.dot_general(
            weighted[64 * j:64 * j + 64], acc_a[64 * j:64 * j + 64, :], (((0,), (0,)), ((), ())),
            precision=lax.Precision.HIGHEST, preferred_element_type=F32) * 0.125

    def p2_copy(k):
        dest = ahead(r, k)
        return remote(p2s.at[:, pl.ds(pl.multiple_of(dest * 16, 16), 16), :], p2r.at[r],
                      p2ss.at[k], p2rs.at[k], to_row(dest))

    def p2_wait(k):
        return remote(p2s.at[:, pl.ds(0, 16), :], p2r.at[behind(r, k)], p2ss.at[k], p2rs.at[k],
                      to_row(ahead(r, k)))

    def p2_send(k, _):
        p2_copy(k).start()
        return 0
    lax.fori_loop(1, 8, p2_send, 0)
    p2r[r] = p2s[:, pl.ds(pl.multiple_of(r * 16, 16), 16), :]

    def p2_recv(k, _):
        p2_wait(k).wait_recv()
        return 0
    lax.fori_loop(1, 8, p2_recv, 0)

    pack(p3.at[c], 0, p2r[...].reshape(256, 128), 256)

    def gather(buf, slot_of, ss, rs, fss, frs, use):
        mine = slot_of(q, core)

        def first(k):
            return remote(buf.at[mine], buf.at[mine], ss.at[k], rs.at[k], to_chip(ahead(q, k)))

        def arrives(k):
            slot = slot_of(behind(q, k), core)
            return remote(buf.at[slot], buf.at[slot], ss.at[k], rs.at[k], to_chip(ahead(q, k)))

        def onward(k, which):
            slot = slot_of(behind(q, k), which)
            return remote(buf.at[slot], buf.at[slot], fss.at[k], frs.at[k], to_sib)

        def go(k, _):
            first(k).start()
            return 0
        lax.fori_loop(1, 8, go, 0)
        onward(0, core).start()
        use(mine)

        def near(k, _):
            arrives(k).wait_recv()
            onward(k, core).start()
            use(slot_of(behind(q, k), core))
            return 0
        lax.fori_loop(1, 8, near, 0)

        def far(k, _):
            onward(k, 1 - core).wait_recv()
            use(slot_of(behind(q, k), 1 - core))
            return 0
        lax.fori_loop(0, 8, far, 0)

        def finish():
            def done(k, _):
                first(k).wait_send()
                return 0
            lax.fori_loop(1, 8, done, 0)

            def done_on(k, _):
                onward(k, core).wait_send()
                return 0
            lax.fori_loop(0, 8, done_on, 0)
        return finish

    def use3(slot):
        gf[pl.ds(pl.multiple_of(slot * 256, 256), 256), :] = unpack(p3.at[slot], 0, 256, 256)

    finish3 = gather(p3, lambda chip, k: chip * 2 + k, p3ss, p3rs, f3ss, f3rs, use3)

    onehot = (lax.broadcasted_iota(jnp.int32, (128, 256), 0) == ids[...]).astype(F32).astype(BF16)

    def fold(o, _):
        hi, lo = split(gf[pl.ds(o, 256, stride=16), :])
        hi, lo = split(dot(onehot, hi) + dot(onehot, lo))
        lanes = pl.ds(pl.multiple_of(o * 128, 128), 128)
        amat[0:128, lanes] = hi
        amat[128:256, lanes] = lo
        return 0
    lax.fori_loop(0, 16, fold, 0)

    def p4_copy(dest):
        return remote(p4s.at[dest], p4r.at[r], p4ss.at[dest], p4rs.at[r], to_row(dest))

    def p4_wait(src):
        return remote(p4s.at[src], p4r.at[src], p4ss.at[src], p4rs.at[src], to_row(src))

    def precondition(k, _):
        p = (r // 2 + k) % 4
        lanes = pl.ds(pl.multiple_of(p * 256, 256), 256)
        both = dot(amat[...], fhi[:, lanes])
        full = both[0:128] + both[128:256] + dot(amat[0:128, :], flo[:, lanes])
        for e in range(2):
            dest = 2 * p + e
            part = full[:, e * 128:(e + 1) * 128]
            pack(p4s.at[dest], 0, part, 128)

            @pl.when(dest != r)
            def _():
                p4_copy(dest).start()

            @pl.when(dest == r)
            def _():
                acc4[...] = part
        return 0
    lax.fori_loop(1, 5, precondition, 0)

    def p4_recv(k, _):
        src = behind(r, k)
        p4_wait(src).wait_recv()
        acc4[...] += unpack(p4r.at[src], 0, 128, 128)
        return 0
    lax.fori_loop(1, 8, p4_recv, 0)

    mine5 = pl.ds(pl.multiple_of(r * 128, 128), 128)
    p5[mine5, :] = acc4[...].T.astype(BF16)

    def p5_copy(k):
        return remote(p5.at[mine5, :], p5.at[mine5, :], p5ss.at[k], p5rs.at[k], to_row(ahead(r, k)))

    def p5_wait(k):
        rows = pl.ds(pl.multiple_of(behind(r, k) * 128, 128), 128)
        return remote(p5.at[rows, :], p5.at[rows, :], p5ss.at[k], p5rs.at[k], to_row(ahead(r, k)))

    def p5_send(k, _):
        p5_copy(k).start()
        return 0
    lax.fori_loop(1, 8, p5_send, 0)
    store_copy.wait()

    def p5_recv(k, _):
        p5_wait(k).wait_recv()
        return 0
    lax.fori_loop(1, 8, p5_recv, 0)

    def score(half, chip):
        rows = pl.ds(pl.multiple_of(half * 2048 + chip * 256, 256), 256)
        return dot(sv[rows, :], p5[...])

    def p6_copy(k):
        return remote(p6s.at[k], p6r.at[k], p6ss.at[k], p6rs.at[k], to_sib)

    def p6_send(i, _):
        k = i % 8
        pack(p6s.at[k], 0, score(1 - core, ahead(q, k)), 256)
        p6_copy(k).start()
        return 0
    lax.fori_loop(1, 9, p6_send, 0)

    def p7_copy(k):
        return remote(p7s.at[k], p7r.at[k], p7ss.at[k], p7rs.at[k], to_chip(ahead(q, k)))

    def chip_sum(k):
        x = score(core, ahead(q, k))
        p6_copy(k).wait_recv()
        return x + unpack(p6r.at[k], 0, 256, 256)

    def p7_send(k, _):
        pack(p7s.at[k], 0, chip_sum(k), 256)
        p7_copy(k).start()
        return 0
    lax.fori_loop(1, 8, p7_send, 0)
    acc7[...] = chip_sum(0)

    def p7_recv(k, _):
        p7_copy(k).wait_recv()
        acc7[...] += unpack(p7r.at[k], 0, 256, 256)
        return 0
    lax.fori_loop(1, 8, p7_recv, 0)

    pack(ob.at[core * 8 + q], 0, acc7[...], 256)

    def leave(slot):
        return pltpu.make_async_copy(ob.at[slot], out.at[slot], ldo.at[slot])

    finish8 = gather(ob, lambda chip, k: k * 8 + chip, p8ss, p8rs, f8ss, f8rs, lambda slot: leave(slot).start())

    def done(k, _):
        p1_copy(k).wait_send()
        p2_wait(k).wait_send()
        p4_wait(ahead(r, k)).wait_send()
        p5_copy(k).wait_send()
        p7_copy(k).wait_send()
        return 0
    lax.fori_loop(1, 8, done, 0)

    def done6(k, _):
        p6_copy(k).wait_send()
        return 0
    lax.fori_loop(0, 8, done6, 0)
    finish3()
    finish8()

    def done_out(k, _):
        leave(k).wait()
        return 0
    lax.fori_loop(0, 16, done_out, 0)


def local(activations, out_grads, proj_in, proj_out, fisher_inv, store, lengths, judge_ids):
    br_here, toks, width = activations.shape
    any_spec = pl.BlockSpec(memory_space=pl.ANY)
    dma = pltpu.SemaphoreType.DMA
    coded = pl.pallas_call(
        kernel,
        out_shape=jax.ShapeDtypeStruct((16, 272, 128), BF16),
        in_specs=[any_spec] * 6 + [pl.BlockSpec(memory_space=pltpu.SMEM), pl.BlockSpec(memory_space=pltpu.VMEM)],
        out_specs=any_spec,
        scratch_shapes=[
            pltpu.VMEM((1024, 1024), BF16), pltpu.VMEM((1024, 1024), BF16),
            pltpu.VMEM((1024, 128), BF16), pltpu.VMEM((1024, 128), BF16),
            pltpu.VMEM((2048, 1024), F32), pltpu.VMEM((2048, 1024), BF16), pltpu.VMEM((2048, 1024), BF16),
            pltpu.VMEM((4096, 1024), BF16),
            pltpu.VMEM((8, 288, 128), BF16), pltpu.VMEM((8, 288, 128), BF16),
            pltpu.VMEM((128, 128), F32), pltpu.VMEM((128, 128), F32),
            pltpu.VMEM((2, 128, 128), F32), pltpu.VMEM((8, 2, 16, 128), F32),
            pltpu.VMEM((16, 272, 128), BF16), pltpu.VMEM((4096, 128), F32), pltpu.VMEM((256, 2048), BF16),
            pltpu.VMEM((8, 144, 128), BF16), pltpu.VMEM((8, 144, 128), BF16), pltpu.VMEM((128, 128), F32),
            pltpu.VMEM((1024, 128), BF16),
            pltpu.VMEM((8, 272, 128), BF16), pltpu.VMEM((8, 272, 128), BF16),
            pltpu.VMEM((8, 272, 128), BF16), pltpu.VMEM((8, 272, 128), BF16),
            pltpu.VMEM((256, 128), F32), pltpu.VMEM((16, 272, 128), BF16),
            dma((2, 9)), dma((2,)), dma((8,)), dma(()), dma((16,)),
        ] + [dma((8,)) for _ in range(20)],
        compiler_params=pltpu.CompilerParams(
            collective_id=0, has_side_effects=True, vmem_limit_bytes=56 * 1024 * 1024),
    )(activations.reshape(br_here * toks, width), out_grads.reshape(br_here * toks, width),
      proj_in, proj_out, fisher_inv, store, lengths, judge_ids.reshape(1, -1))
    return decode(coded[:, :256, :], coded[:, 256:257, :].astype(F32)).reshape(4096, 128)


def solution(mesh):
    placed = (
        P(("grp", "col"), None, "row"),
        P(("grp", "col"), None, "row"),
        P("row", None),
        P("row", None),
        P("row", ("grp", "col")),
        P("row", ("grp", "col")),
        P(("grp", "col")),
        P(),
    )
    return jax.shard_map(
        local, mesh=mesh, in_specs=placed, out_specs=P("row", None), check_vma=False
    )
```

```python
import jax
import jax.numpy as jnp
from jax import lax
from jax.experimental import pallas as pl
from jax.experimental.pallas import tpu as pltpu
from jax.sharding import PartitionSpec as P

MESH = pl.DeviceIdType.MESH
F32 = jnp.float32
BF16 = jnp.bfloat16
SPAN = 80.0


def bound(x):
    top = jnp.max(jnp.abs(x), axis=0, keepdims=True)
    return (top * 1.01 + 1e-36).astype(BF16)


def encode(x, m):
    y = jnp.exp(jnp.abs(x) * (SPAN / m) - 0.5 * SPAN)
    return jnp.where(x < 0, -y, y).astype(BF16)


def decode(y, m):
    y = y.astype(F32)
    t = (jnp.log(jnp.abs(y)) + 0.5 * SPAN) * (m / SPAN)
    return jnp.where(y < 0, -t, t)


def pack(ref, x):
    rows = x.shape[0]
    m = bound(x)
    ref[0:rows, :] = encode(x, m.astype(F32))
    ref[rows:rows + 16, :] = jnp.broadcast_to(m, (16, x.shape[1]))


def unpack(ref):
    rows = ref.shape[0] - 16
    return decode(ref[0:rows, :], ref[rows:rows + 16, :][:1].astype(F32))


def split(x):
    hi = x.astype(BF16)
    return hi, (x - hi.astype(F32)).astype(BF16)


def dot(a, b):
    return jnp.dot(a, b, preferred_element_type=F32)


def loop(lo, hi, body):
    def step(i, _):
        body(i)
        return 0
    lax.fori_loop(lo, hi, step, 0)


def kernel(
    act, og, pin, pout, fish, store, lens, ids, out,
    actv, ogv, pinv, poutv, fv, fhi, flo, sv,
    proj, p1s, p1r, acc1, p2s, p2r, p3, gf, amat,
    p4s, p4r, acc4, p5, pre, p6s, p6r, p7s, p7r, acc7, ob,
    ldw, ld1, ldf, lds, ldo,
    p1ss, p1rs, p2ss, p2rs, p3ss, p3rs, f3ss, f3rs, p4ss, p4rs, p5ss, p5rs,
    p6ss, p6rs, p7ss, p7rs, p8ss, p8rs, f8ss, f8rs,
):
    g = lax.axis_index("grp")
    r = lax.axis_index("row")
    col = lax.axis_index("col")
    y, core = lax.div(col, 2), lax.rem(col, 2)
    q = g * 4 + y
    sib = col + 1 - 2 * core
    rx, rz = lax.div(r, 4), lax.rem(r, 4)
    peers = range(1, 8)
    both = range(2)

    def around(hi, lo, k, sign):
        return lax.rem(hi + k // 4, 2) * 4 + lax.rem(lo + (k % 4 if sign > 0 else 4 - k % 4), 4)

    row_to = [around(rx, rz, k, 1) for k in range(8)]
    row_from = [around(rx, rz, k, -1) for k in range(8)]
    chip_to = [around(g, y, k, 1) for k in range(8)]
    chip_from = [around(g, y, k, -1) for k in range(8)]
    to_row = [{"row": i} for i in row_to]
    to_chip = [{"grp": lax.rem(g + k // 4, 2), "col": lax.rem(y + k % 4, 4) * 2 + core} for k in range(8)]
    to_sib = {"col": sib}

    def remote(src, dst, ss, rs, dev):
        return pltpu.make_async_remote_copy(
            src_ref=src, dst_ref=dst, send_sem=ss, recv_sem=rs, device_id=dev, device_id_type=MESH)

    load_w = [pltpu.make_async_copy(pin, pinv, ldw.at[0]), pltpu.make_async_copy(pout, poutv, ldw.at[1])]

    def load_tokens(h, which):
        rows = pl.ds(512 * h, 512)
        src, dst = ((act, actv), (og, ogv))[which]
        return pltpu.make_async_copy(src.at[rows, :], dst.at[rows, :], ld1.at[h, which])

    load_w[0].start()
    load_tokens(0, 0).start()
    load_w[1].start()
    load_tokens(0, 1).start()
    load_tokens(1, 0).start()
    load_tokens(1, 1).start()
    barrier = pltpu.get_barrier_semaphore()
    for k in peers:
        pl.semaphore_signal(barrier, inc=1, device_id=to_row[k], device_id_type=MESH)
        pl.semaphore_signal(barrier, inc=1, device_id=to_chip[k], device_id_type=MESH)
    pl.semaphore_signal(barrier, inc=1, device_id=to_sib, device_id_type=MESH)

    def f_load(i):
        rows = pl.ds(pl.multiple_of(i * 256, 256), 256)
        return pltpu.make_async_copy(fish.at[rows, :], fv.at[rows, :], ldf.at[i])

    def f_split(i):
        f_load(i).wait()

        def part(j):
            rows = pl.ds(pl.multiple_of(i * 256 + j * 32, 32), 32)
            hi, lo = split(fv[rows, :])
            fhi[rows, :] = hi
            flo[rows, :] = lo
        loop(0, 8, part)

    def p1_copy(h, k):
        return remote(p1s.at[h, k], p1r.at[h, k], p1ss.at[h, k], p1rs.at[h, k], to_row[k])

    for h in both:
        rows = slice(512 * h, 512 * h + 512)
        if h == 0:
            load_w[0].wait()
        load_tokens(h, 0).wait()
        proj[:, 0:128] = dot(actv[rows, :], pinv[...])
        if h == 0:
            load_w[1].wait()
        load_tokens(h, 1).wait()
        proj[:, 128:256] = dot(ogv[rows, :], poutv[...])
        for k in peers:
            pack(p1s.at[h, k], proj[pl.ds(pl.multiple_of(row_to[k] * 64, 64), 64), :])
            if h == 0 and k == 1:
                pl.semaphore_wait(barrier, 15)
            p1_copy(h, k).start()
        acc1[h] = proj[pl.ds(pl.multiple_of(r * 64, 64), 64), :]

    loop(0, 8, lambda i: f_load(i).start())
    onehot = (lax.broadcasted_iota(jnp.int32, (128, 256), 0) == ids[...]).astype(F32).astype(BF16)
    place = (lax.broadcasted_iota(jnp.int32, (256, 256), 0), lax.broadcasted_iota(jnp.int32, (256, 256), 1))
    moved = lax.rem(lax.div(place[1], 8), 16) * 16 + lax.div(place[1], 128) * 8 + lax.rem(place[1], 8)
    onehot = dot(onehot, (place[0] == moved).astype(F32).astype(BF16)).astype(BF16)
    loop(0, 5, f_split)

    def p2_copy(h, k):
        rows = pl.ds(pl.multiple_of(row_to[k] * 16, 16), 16)
        return remote(p2s.at[h, rows, :], p2r.at[h, pl.ds(pl.multiple_of(r * 16, 16), 16), :],
                      p2ss.at[h, k], p2rs.at[h, k], to_row[k])

    def p2_arrive(h, k):
        rows = pl.ds(pl.multiple_of(row_from[k] * 16, 16), 16)
        return remote(p2s.at[h, rows, :], p2r.at[h, rows, :], p2ss.at[h, k], p2rs.at[h, k], to_row[k])

    for h in both:
        for k in peers:
            p1_copy(h, k).wait_recv()
            acc1[h] += unpack(p1r.at[h, k])
        total = acc1[h]
        live = lax.broadcasted_iota(jnp.int32, (64, 128), 0) < lens[8 * h + r]
        ahi, alo = split(total[:, 0:128])
        ghi, glo = split(jnp.where(live, total[:, 128:256], 0.0) * 0.125)
        p2s[h] = lax.dot_general(
            jnp.concatenate([ghi, ghi, glo], axis=0), jnp.concatenate([ahi, alo, ahi], axis=0),
            (((0,), (0,)), ((), ())), preferred_element_type=F32)
        for k in peers:
            p2_copy(h, k).start()
        own = pl.ds(pl.multiple_of(r * 16, 16), 16)
        p2r[h, own, :] = p2s[h, own, :]
    store_copy = pltpu.make_async_copy(store, sv, lds)
    store_copy.start()
    loop(5, 8, f_split)

    def slot3(chip, k):
        return chip * 2 + k

    mine3 = slot3(q, core)

    def p3_copy(h, k):
        return remote(p3.at[h, mine3], p3.at[h, mine3], p3ss.at[h, k], p3rs.at[h, k], to_chip[k])

    def p3_arrive(h, k):
        slot = slot3(chip_from[k], core)
        return remote(p3.at[h, slot], p3.at[h, slot], p3ss.at[h, k], p3rs.at[h, k], to_chip[k])

    def p3_onward(h, k, which):
        slot = slot3(chip_from[k], which)
        return remote(p3.at[h, slot], p3.at[h, slot], f3ss.at[h, k], f3rs.at[h, k], to_sib)

    def use3(h, slot):
        x = unpack(p3.at[h, slot])
        rows = pl.ds(pl.multiple_of(h * 128 + slot * 8, 8), 8)
        for o in range(16):
            gf[o // 2, rows, (o % 2) * 128:(o % 2) * 128 + 128] = x[8 * o:8 * o + 8]

    for h in both:
        for k in peers:
            p2_arrive(h, k).wait_recv()
        pack(p3.at[h, mine3], jnp.concatenate([p2r[h, pl.ds(o, 8, stride=16), :] for o in range(16)], axis=0))
        for k in peers:
            p3_copy(h, k).start()
        p3_onward(h, 0, core).start()
        use3(h, mine3)
    for h in both:
        for k in peers:
            p3_arrive(h, k).wait_recv()
            p3_onward(h, k, core).start()
            use3(h, slot3(chip_from[k], core))
        for k in range(8):
            p3_onward(h, k, 1 - core).wait_recv()
            use3(h, slot3(chip_from[k], 1 - core))

    for j in range(8):
        hi, lo = split(gf[j])
        hi, lo = split(dot(onehot, hi) + dot(onehot, lo))
        amat[0:128, 256 * j:256 * j + 256] = hi
        amat[128:256, 256 * j:256 * j + 256] = lo

    def p4_copy(dest):
        return remote(p4s.at[dest], p4r.at[r], p4ss.at[dest], p4rs.at[r], {"row": dest})

    def p4_arrive(k):
        src = row_from[k]
        return remote(p4s.at[src], p4r.at[src], p4ss.at[src], p4rs.at[src], to_row[k])

    def precondition(k):
        p = lax.rem(lax.div(r, 2) + k, 4)
        lanes = pl.ds(pl.multiple_of(p * 256, 256), 256)
        two = dot(amat[...], fhi[:, lanes])
        full = two[0:128] + two[128:256] + dot(amat[0:128, :], flo[:, lanes])
        for e in both:
            dest = 2 * p + e
            part = full[:, e * 128:(e + 1) * 128]
            pack(p4s.at[dest], part)

            @pl.when(dest != r)
            def _():
                p4_copy(dest).start()

            @pl.when(dest == r)
            def _():
                acc4[...] = part
    loop(1, 5, precondition)

    for k in peers:
        p4_arrive(k).wait_recv()
        acc4[...] += unpack(p4r.at[row_from[k]])

    def p5_copy(k):
        return remote(p5.at[r], p5.at[r], p5ss.at[k], p5rs.at[k], to_row[k])

    def p5_arrive(k):
        return remote(p5.at[row_from[k]], p5.at[row_from[k]], p5ss.at[k], p5rs.at[k], to_row[k])

    def use5(i, x):
        hi, lo = split(x)
        rows = pl.ds(pl.multiple_of(i * 128, 128), 128)
        pre[rows, 0:128] = hi
        pre[rows, 128:256] = lo

    own5 = acc4[...].T
    pack(p5.at[r], own5)
    for k in peers:
        p5_copy(k).start()
    use5(r, own5)
    store_copy.wait()
    for k in peers:
        for h in both:
            p1_copy(h, k).wait_send()
            p2_copy(h, k).wait_send()
    for k in peers:
        p5_arrive(k).wait_recv()
        use5(row_from[k], unpack(p5.at[row_from[k]]))

    def score(half, pair):
        rows = pl.ds(pl.multiple_of(half * 2048 + pair * 512, 512), 512)
        two = dot(sv[rows, :], pre[...])
        return two[:, 0:128] + two[:, 128:256]

    def p6_copy(t):
        return remote(p6s.at[t], p6r.at[t], p6ss.at[t], p6rs.at[t], to_sib)

    def p6_send(k):
        t = lax.rem(lax.div(q, 2) + k, 4)
        p6s[t] = score(1 - core, t)
        p6_copy(t).start()
    loop(1, 5, p6_send)

    def p7_copy(dest):
        return remote(p7s.at[dest], p7r.at[q], p7ss.at[dest], p7rs.at[q],
                      {"grp": lax.div(dest, 4), "col": lax.rem(dest, 4) * 2 + core})

    def p7_arrive(k):
        src = chip_from[k]
        return remote(p7s.at[src], p7r.at[src], p7ss.at[src], p7rs.at[src], to_chip[k])

    def p7_send(k):
        t = lax.rem(lax.div(q, 2) + k, 4)
        x = score(core, t)
        p6_copy(t).wait_recv()
        x = x + p6r[t]
        for e in both:
            dest = 2 * t + e
            part = x[256 * e:256 * e + 256]
            pack(p7s.at[dest], part)

            @pl.when(dest != q)
            def _():
                p7_copy(dest).start()

            @pl.when(dest == q)
            def _():
                acc7[...] = part
    loop(1, 5, p7_send)

    for k in peers:
        p4_copy(row_to[k]).wait_send()
        p5_copy(k).wait_send()
        for h in both:
            p3_copy(h, k).wait_send()
    for k in range(8):
        for h in both:
            p3_onward(h, k, core).wait_send()

    for k in peers:
        p7_arrive(k).wait_recv()
        acc7[...] += unpack(p7r.at[chip_from[k]])

    def place8(chip, which):
        return pl.ds(pl.multiple_of(which * 2048 + chip * 256, 256), 256)

    mine8 = place8(q, core)
    ob[mine8, :] = acc7[...].astype(BF16)

    def p8_copy(k):
        return remote(ob.at[mine8, :], ob.at[mine8, :], p8ss.at[k], p8rs.at[k], to_chip[k])

    def p8_arrive(k):
        rows = place8(chip_from[k], core)
        return remote(ob.at[rows, :], ob.at[rows, :], p8ss.at[k], p8rs.at[k], to_chip[k])

    def p8_onward(k, which):
        rows = place8(chip_from[k], which)
        return remote(ob.at[rows, :], ob.at[rows, :], f8ss.at[k], f8rs.at[k], to_sib)

    def leave(k, which):
        rows = place8(chip_from[k], which)
        return pltpu.make_async_copy(ob.at[rows, :], out.at[rows, :], ldo.at[k, which])

    for k in peers:
        p8_copy(k).start()
    p8_onward(0, core).start()
    leave(0, core).start()
    for k in peers:
        p7_copy(chip_to[k]).wait_send()
    loop(0, 4, lambda t: p6_copy(t).wait_send())
    for k in peers:
        p8_arrive(k).wait_recv()
        p8_onward(k, core).start()
        leave(k, core).start()
    for k in range(8):
        p8_onward(k, 1 - core).wait_recv()
        leave(k, 1 - core).start()
    for k in peers:
        p8_copy(k).wait_send()
    for k in range(8):
        p8_onward(k, core).wait_send()
        leave(k, core).wait()
        leave(k, 1 - core).wait()


def local(activations, out_grads, proj_in, proj_out, fisher_inv, store, lengths, judge_ids):
    br_here, toks, width = activations.shape
    any_spec = pl.BlockSpec(memory_space=pl.ANY)
    dma = pltpu.SemaphoreType.DMA
    vmem = pltpu.VMEM
    sums = pl.pallas_call(
        kernel,
        out_shape=jax.ShapeDtypeStruct((4096, 128), BF16),
        in_specs=[any_spec] * 6 + [pl.BlockSpec(memory_space=pltpu.SMEM), pl.BlockSpec(memory_space=pltpu.VMEM)],
        out_specs=any_spec,
        scratch_shapes=[
            vmem((1024, 1024), BF16), vmem((1024, 1024), BF16), vmem((1024, 128), BF16), vmem((1024, 128), BF16),
            vmem((2048, 1024), F32), vmem((2048, 1024), BF16), vmem((2048, 1024), BF16), vmem((4096, 1024), BF16),
            vmem((512, 256), F32), vmem((2, 8, 80, 256), BF16), vmem((2, 8, 80, 256), BF16), vmem((2, 64, 256), F32),
            vmem((2, 128, 128), F32), vmem((2, 128, 128), F32), vmem((2, 16, 144, 128), BF16),
            vmem((8, 256, 256), F32), vmem((256, 2048), BF16),
            vmem((8, 144, 128), BF16), vmem((8, 144, 128), BF16), vmem((128, 128), F32),
            vmem((8, 144, 128), BF16), vmem((1024, 256), BF16),
            vmem((4, 512, 128), F32), vmem((4, 512, 128), F32),
            vmem((8, 272, 128), BF16), vmem((8, 272, 128), BF16), vmem((256, 128), F32), vmem((4096, 128), BF16),
            dma((2,)), dma((2, 2)), dma((8,)), dma(()), dma((8, 2)),
            *[dma((2, 8)) for _ in range(8)], *[dma((8,)) for _ in range(4)],
            *[dma((4,)) for _ in range(2)], *[dma((8,)) for _ in range(6)],
        ],
        compiler_params=pltpu.CompilerParams(
            collective_id=0, has_side_effects=True, vmem_limit_bytes=56 * 1024 * 1024),
    )(activations.reshape(br_here * toks, width), out_grads.reshape(br_here * toks, width),
      proj_in, proj_out, fisher_inv, store, lengths, judge_ids.reshape(1, -1))
    return sums.astype(F32)


def solution(mesh):
    placed = (
        P(("grp", "col"), None, "row"),
        P(("grp", "col"), None, "row"),
        P("row", None),
        P("row", None),
        P("row", ("grp", "col")),
        P("row", ("grp", "col")),
        P(("grp", "col")),
        P(),
    )
    return jax.shard_map(
        local, mesh=mesh, in_specs=placed, out_specs=P("row", None), check_vma=False
    )
```

```python
import jax
import jax.numpy as jnp
from jax import lax
from jax.experimental import pallas as pl
from jax.experimental.pallas import tpu as pltpu
from jax.sharding import PartitionSpec as P

MESH = pl.DeviceIdType.MESH
SENDS = (6, 5, 7, 2, 4, 1, 3)
WAITS = (1, 3, 4, 2, 5, 7, 6)
F32 = jnp.float32
BF16 = jnp.bfloat16
SPAN = 80.0


def bound(x):
    top = jnp.max(jnp.abs(x), axis=0, keepdims=True)
    return (top * 1.01 + 1e-36).astype(BF16)


def encode(x, m):
    y = jnp.exp(jnp.abs(x) * (SPAN / m) - 0.5 * SPAN)
    return jnp.where(x < 0, -y, y).astype(BF16)


def decode(y, m):
    y = y.astype(F32)
    t = (jnp.log(jnp.abs(y)) + 0.5 * SPAN) * (m / SPAN)
    return jnp.where(y < 0, -t, t)


def pack(ref, x):
    rows = x.shape[0]
    m = bound(x)
    ref[0:rows, :] = encode(x, m.astype(F32))
    ref[rows:rows + 16, :] = jnp.broadcast_to(m, (16, x.shape[1]))


def unpack(ref):
    rows = ref.shape[0] - 16
    return decode(ref[0:rows, :], ref[rows:rows + 16, :][:1].astype(F32))


def split(x):
    hi = x.astype(BF16)
    return hi, (x - hi.astype(F32)).astype(BF16)


def dot(a, b):
    return jnp.dot(a, b, preferred_element_type=F32)


def loop(lo, hi, body):
    def step(i, _):
        body(i)
        return 0
    lax.fori_loop(lo, hi, step, 0)


def kernel(
    act, og, pin, pout, fish, store, lens_in, ids_in, out,
    lens, ids, actv, ogv, pinv, poutv, fv, fhi, flo, sv,
    proj, p1s, p1r, acc1, p2s, p2r, p3, gf, amat,
    p4s, p4r, acc4, p5, pre, p6s, p6r, xs, p7s, p7r, acc7, ob,
    ldi, ldw, ld1, ldf, lds, ldo,
    p1ss, p1rs, p2ss, p2rs, p3ss, p3rs, f3ss, f3rs, p4ss, p4rs, p5ss, p5rs,
    p6ss, p6rs, p7ss, p7rs, p8ss, p8rs, f8ss, f8rs,
):
    g = lax.axis_index("grp")
    r = lax.axis_index("row")
    col = lax.axis_index("col")
    y, core = lax.div(col, 2), lax.rem(col, 2)
    q = g * 4 + y
    sib = col + 1 - 2 * core
    rx, rz = lax.div(r, 4), lax.rem(r, 4)
    peers = range(1, 8)
    both = range(2)

    def around(hi, lo, k, sign):
        return lax.rem(hi + k // 4, 2) * 4 + lax.rem(lo + (k % 4 if sign > 0 else 4 - k % 4), 4)

    row_to = [around(rx, rz, k, 1) for k in range(8)]
    row_from = [around(rx, rz, k, -1) for k in range(8)]
    chip_to = [around(g, y, k, 1) for k in range(8)]
    chip_from = [around(g, y, k, -1) for k in range(8)]
    to_row = [{"row": i} for i in row_to]
    to_chip = [{"grp": lax.rem(g + k // 4, 2), "col": lax.rem(y + k % 4, 4) * 2 + core} for k in range(8)]
    to_sib = {"col": sib}

    def remote(src, dst, ss, rs, dev):
        return pltpu.make_async_remote_copy(
            src_ref=src, dst_ref=dst, send_sem=ss, recv_sem=rs, device_id=dev, device_id_type=MESH)

    load_w = [pltpu.make_async_copy(pin, pinv, ldw.at[0]), pltpu.make_async_copy(pout, poutv, ldw.at[1])]

    def load_tokens(h, which):
        rows = pl.ds(512 * h, 512)
        src, dst = ((act, actv), (og, ogv))[which]
        return pltpu.make_async_copy(src.at[rows, :], dst.at[rows, :], ld1.at[h, which])

    load_w[0].start()
    load_tokens(0, 0).start()
    load_w[1].start()
    load_tokens(0, 1).start()
    barrier = pltpu.get_barrier_semaphore()
    for k in peers:
        pl.semaphore_signal(barrier, inc=1, device_id=to_row[k], device_id_type=MESH)
        pl.semaphore_signal(barrier, inc=1, device_id=to_chip[k], device_id_type=MESH)
    pl.semaphore_signal(barrier, inc=1, device_id=to_sib, device_id_type=MESH)
    load_tokens(1, 0).start()
    load_tokens(1, 1).start()
    load_lens = pltpu.make_async_copy(lens_in, lens, ldi.at[0])
    load_ids = pltpu.make_async_copy(ids_in, ids, ldi.at[1])
    load_lens.start()
    load_ids.start()

    def f_load(i):
        rows = pl.ds(pl.multiple_of(i * 256, 256), 256)
        return pltpu.make_async_copy(fish.at[rows, :], fv.at[rows, :], ldf.at[i])

    def f_split(i):
        f_load(i).wait()

        def part(j):
            rows = pl.ds(pl.multiple_of(i * 256 + j * 32, 32), 32)
            hi, lo = split(fv[rows, :])
            fhi[rows, :] = hi
            flo[rows, :] = lo
        loop(0, 8, part)

    def p1_copy(h, k):
        return remote(p1s.at[h, k], p1r.at[h, k], p1ss.at[h, k], p1rs.at[h, k], to_row[k])

    for h in both:
        rows = slice(512 * h, 512 * h + 512)
        if h == 0:
            load_w[0].wait()
        load_tokens(h, 0).wait()
        proj[:, 0:128] = dot(actv[rows, :], pinv[...])
        if h == 0:
            load_w[1].wait()
        load_tokens(h, 1).wait()
        proj[:, 128:256] = dot(ogv[rows, :], poutv[...])
        for k in SENDS:
            x = proj[pl.ds(pl.multiple_of(row_to[k] * 64, 64), 64), :]
            m = bound(x)
            code = encode(x, m.astype(F32))
            p1s[h, k, 0:64] = code[:, 0:128]
            p1s[h, k, 64:128] = code[:, 128:256]
            p1s[h, k, 128:144] = jnp.concatenate(
                [jnp.broadcast_to(m[:, 0:128], (8, 128)), jnp.broadcast_to(m[:, 128:256], (8, 128))], axis=0)
            if h == 0 and k == SENDS[0]:
                pl.semaphore_wait(barrier, 15)
            p1_copy(h, k).start()
        acc1[h] = proj[pl.ds(pl.multiple_of(r * 64, 64), 64), :]

    loop(0, 8, lambda i: f_load(i).start())
    load_lens.wait()
    load_ids.wait()
    onehot = (lax.broadcasted_iota(jnp.int32, (128, 256), 0) == ids[...]).astype(F32).astype(BF16)
    place = (lax.broadcasted_iota(jnp.int32, (256, 256), 0), lax.broadcasted_iota(jnp.int32, (256, 256), 1))
    moved = lax.rem(lax.div(place[1], 8), 16) * 16 + lax.div(place[1], 128) * 8 + lax.rem(place[1], 8)
    onehot = dot(onehot, (place[0] == moved).astype(F32).astype(BF16)).astype(BF16)
    loop(0, 5, f_split)

    def p2_copy(h, k):
        rows = pl.ds(pl.multiple_of(row_to[k] * 16, 16), 16)
        return remote(p2s.at[h, rows, :], p2r.at[h, pl.ds(pl.multiple_of(r * 16, 16), 16), :],
                      p2ss.at[h, k], p2rs.at[h, k], to_row[k])

    def p2_arrive(h, k):
        rows = pl.ds(pl.multiple_of(row_from[k] * 16, 16), 16)
        return remote(p2s.at[h, rows, :], p2r.at[h, rows, :], p2ss.at[h, k], p2rs.at[h, k], to_row[k])

    for h in both:
        for k in WAITS:
            p1_copy(h, k).wait_recv()
            m = p1r[h, k, 128:144].astype(F32)
            acc1[h, :, 0:128] += decode(p1r[h, k, 0:64], m[0:1])
            acc1[h, :, 128:256] += decode(p1r[h, k, 64:128], m[8:9])
        total = acc1[h]
        live = lax.broadcasted_iota(jnp.int32, (64, 128), 0) < lens[8 * h + r]
        ahi, alo = split(total[:, 0:128])
        ghi, glo = split(jnp.where(live, total[:, 128:256], 0.0) * 0.125)
        p2s[h] = lax.dot_general(
            jnp.concatenate([ghi, ghi, glo], axis=0), jnp.concatenate([ahi, alo, ahi], axis=0),
            (((0,), (0,)), ((), ())), preferred_element_type=F32)
        for k in SENDS:
            p2_copy(h, k).start()
        own = pl.ds(pl.multiple_of(r * 16, 16), 16)
        p2r[h, own, :] = p2s[h, own, :]
    store_copy = pltpu.make_async_copy(store, sv, lds)
    store_copy.start()
    loop(5, 8, f_split)

    def slot3(chip, k):
        return chip * 2 + k

    mine3 = slot3(q, core)

    def p3_copy(h, k):
        return remote(p3.at[h, mine3], p3.at[h, mine3], p3ss.at[h, k], p3rs.at[h, k], to_chip[k])

    def p3_arrive(h, k):
        slot = slot3(chip_from[k], core)
        return remote(p3.at[h, slot], p3.at[h, slot], p3ss.at[h, k], p3rs.at[h, k], to_chip[k])

    def p3_onward(h, k, which):
        slot = slot3(chip_from[k], which)
        return remote(p3.at[h, slot], p3.at[h, slot], f3ss.at[h, k], f3rs.at[h, k], to_sib)

    def use3(h, slot):
        x = unpack(p3.at[h, slot])
        rows = pl.ds(pl.multiple_of(h * 128 + slot * 8, 8), 8)
        for o in range(16):
            gf[o // 2, rows, (o % 2) * 128:(o % 2) * 128 + 128] = x[8 * o:8 * o + 8]

    for h in both:
        for k in peers:
            p2_arrive(h, k).wait_recv()
        pack(p3.at[h, mine3], jnp.concatenate([p2r[h, pl.ds(o, 8, stride=16), :] for o in range(16)], axis=0))
        for k in SENDS:
            p3_copy(h, k).start()
        p3_onward(h, 0, core).start()
        use3(h, mine3)
    for h in both:
        for k in WAITS:
            p3_arrive(h, k).wait_recv()
            p3_onward(h, k, core).start()
            use3(h, slot3(chip_from[k], core))
        for k in (0, *WAITS):
            p3_onward(h, k, 1 - core).wait_recv()
            use3(h, slot3(chip_from[k], 1 - core))

    for j in range(8):
        hi, lo = split(gf[j])
        hi, lo = split(dot(onehot, hi) + dot(onehot, lo))
        amat[0:128, 256 * j:256 * j + 256] = hi
        amat[128:256, 256 * j:256 * j + 256] = lo

    def p4_copy(dest):
        return remote(p4s.at[dest], p4r.at[r], p4ss.at[dest], p4rs.at[r], {"row": dest})

    def p4_arrive(k):
        src = row_from[k]
        return remote(p4s.at[src], p4r.at[src], p4ss.at[src], p4rs.at[src], to_row[k])

    def precondition(k):
        p = lax.rem(rx + 1 - lax.rem(k, 2), 2) * 2 + lax.rem(lax.div(rz, 2) + 1 - lax.div(k, 2), 2)
        lanes = pl.ds(pl.multiple_of(p * 256, 256), 256)
        two = dot(amat[...], fhi[:, lanes])
        full = two[0:128] + two[128:256] + dot(amat[0:128, :], flo[:, lanes])
        for e in both:
            dest = 2 * p + e
            part = full[:, e * 128:(e + 1) * 128]
            pack(p4s.at[dest], part)

            @pl.when(dest != r)
            def _():
                p4_copy(dest).start()

            @pl.when(dest == r)
            def _():
                acc4[...] = part
    loop(0, 4, precondition)

    for k in WAITS:
        p4_arrive(k).wait_recv()
        acc4[...] += unpack(p4r.at[row_from[k]])

    def p5_copy(k):
        return remote(p5.at[r], p5.at[r], p5ss.at[k], p5rs.at[k], to_row[k])

    def p5_arrive(k):
        return remote(p5.at[row_from[k]], p5.at[row_from[k]], p5ss.at[k], p5rs.at[k], to_row[k])

    def use5(i, x):
        hi, lo = split(x)
        rows = pl.ds(pl.multiple_of(i * 128, 128), 128)
        pre[rows, 0:128] = hi
        pre[rows, 128:256] = lo

    own5 = acc4[...].T
    pack(p5.at[r], own5)
    for k in (2, 1, 3, 6, 5, 7, 4):
        p5_copy(k).start()
    use5(r, own5)
    store_copy.wait()
    for k in peers:
        for h in both:
            p1_copy(h, k).wait_send()
            p2_copy(h, k).wait_send()
    def score(half, group, part):
        rows = pl.ds(pl.multiple_of(half * 2048 + group * 1024, 1024), 1024)
        feats = pl.ds(pl.multiple_of(part * 512, 512), 512)
        two = dot(sv[rows, feats], pre[feats, :])
        return two[:, 0:128] + two[:, 128:256]

    for k in (1, 3, 2):
        p5_arrive(k).wait_recv()
        use5(row_from[k], unpack(p5.at[row_from[k]]))

    def score_own(u):
        p6s[u] = score(1 - core, u, rx)
        xs[u] = score(core, u, rx)
    loop(0, 2, score_own)
    for k in (4, 5, 7, 6):
        p5_arrive(k).wait_recv()
        use5(row_from[k], unpack(p5.at[row_from[k]]))

    def p6_copy(u):
        return remote(p6s.at[u], p6r.at[u], p6ss.at[u], p6rs.at[u], to_sib)

    def p6_send(i):
        u = lax.rem(g + 1 + i, 2)
        p6s[u] += score(1 - core, u, 1 - rx)
        p6_copy(u).start()
    loop(0, 2, p6_send)

    parts = (pl.ds(0, 144), pl.ds(144, 128))

    def p7_copy(k, a):
        return remote(p7s.at[k, parts[a]], p7r.at[k, parts[a]], p7ss.at[k, a], p7rs.at[k, a], to_chip[k])

    for i in both:
        u = lax.rem(g + 1 + i, 2)
        xs[u] += score(core, u, 1 - rx)
        p6_copy(u).wait_recv()
        for k in ((6, 5, 7, 4), (2, 1, 3, 0))[i]:
            rows = pl.ds(pl.multiple_of(lax.rem(chip_to[k], 4) * 256, 256), 256)
            x = xs[u, rows, :] + p6r[u, rows, :]
            if k == 0:
                acc7[...] = x
                continue
            m = bound(x)
            code = encode(x, m.astype(F32))
            p7s[k, 0:128] = code[0:128]
            p7s[k, 128:144] = jnp.broadcast_to(m, (16, 128))
            p7s[k, 144:272] = code[128:256]
            p7_copy(k, 0).start()
    for k in SENDS:
        p7_copy(k, 1).start()

    for k in peers:
        p4_copy(row_to[k]).wait_send()
        p5_copy(k).wait_send()
        for h in both:
            p3_copy(h, k).wait_send()
    for k in range(8):
        for h in both:
            p3_onward(h, k, core).wait_send()

    def place8(chip, which, a):
        return pl.ds(pl.multiple_of(which * 2048 + chip * 256 + a * 128, 128), 128)

    def p8_copy(k, a):
        rows = place8(q, core, a)
        return remote(ob.at[rows, :], ob.at[rows, :], p8ss.at[k, a], p8rs.at[k, a], to_chip[k])

    def p8_arrive(k, a):
        rows = place8(chip_from[k], core, a)
        return remote(ob.at[rows, :], ob.at[rows, :], p8ss.at[k, a], p8rs.at[k, a], to_chip[k])

    def p8_onward(k, which, a):
        rows = place8(chip_from[k], which, a)
        return remote(ob.at[rows, :], out.at[rows, :], f8ss.at[k, a], f8rs.at[k, a], to_sib)

    def leave(k, a):
        rows = place8(chip_from[k], core, a)
        return pltpu.make_async_copy(ob.at[rows, :], out.at[rows, :], ldo.at[k, a])

    for a in both:
        half = slice(128 * a, 128 * a + 128)
        for k in WAITS:
            p7_copy(k, a).wait_recv()
            acc7[half] += decode(p7r[k, parts[a]][0:128], p7r[k, 128:144][:1].astype(F32))
        ob[place8(q, core, a), :] = acc7[half].astype(BF16)
        for k in SENDS:
            p8_copy(k, a).start()
        p8_onward(0, core, a).start()
        leave(0, a).start()
    for k in peers:
        for a in both:
            p7_copy(k, a).wait_send()
    loop(0, 2, lambda u: p6_copy(u).wait_send())
    for a in both:
        for k in WAITS:
            p8_arrive(k, a).wait_recv()
            p8_onward(k, core, a).start()
            leave(k, a).start()
    for a in both:
        for k in peers:
            p8_copy(k, a).wait_send()
        for k in range(8):
            p8_onward(k, core, a).wait_send()
            leave(k, a).wait()
    for a in both:
        for k in range(8):
            p8_onward(k, 1 - core, a).wait_recv()


def widen(src, dst, held, wide, got, put):
    count = got.shape[0]
    rows = src.shape[0] // count

    def load(i):
        part = pl.ds(i * rows, rows)
        return pltpu.make_async_copy(src.at[part, :], held.at[part, :], got.at[i])

    def leave(i):
        part = pl.ds(i * rows, rows)
        return pltpu.make_async_copy(wide.at[part, :], dst.at[part, :], put.at[i])

    for i in range(count):
        load(i).start()
    for i in range(count):
        load(i).wait()
        wide[i * rows:(i + 1) * rows] = held[i * rows:(i + 1) * rows].astype(F32)
        leave(i).start()
    for i in range(count):
        leave(i).wait()


def local(activations, out_grads, proj_in, proj_out, fisher_inv, store, lengths, judge_ids):
    br_here, toks, width = activations.shape
    any_spec = pl.BlockSpec(memory_space=pl.ANY)
    dma = pltpu.SemaphoreType.DMA
    vmem = pltpu.VMEM
    sums = pl.pallas_call(
        kernel,
        out_shape=jax.ShapeDtypeStruct((4096, 128), BF16),
        in_specs=[any_spec] * 8,
        out_specs=any_spec,
        scratch_shapes=[
            pltpu.SMEM((16,), jnp.int32), vmem((1, 256), jnp.int32), vmem((1024, 1024), BF16), vmem((1024, 1024), BF16), vmem((1024, 128), BF16), vmem((1024, 128), BF16),
            vmem((2048, 1024), F32), vmem((2048, 1024), BF16), vmem((2048, 1024), BF16), vmem((4096, 1024), BF16),
            vmem((512, 256), F32), vmem((2, 8, 144, 128), BF16), vmem((2, 8, 144, 128), BF16), vmem((2, 64, 256), F32),
            vmem((2, 128, 128), F32), vmem((2, 128, 128), F32), vmem((2, 16, 144, 128), BF16),
            vmem((8, 256, 256), F32), vmem((256, 2048), BF16),
            vmem((8, 144, 128), BF16), vmem((8, 144, 128), BF16), vmem((128, 128), F32),
            vmem((8, 144, 128), BF16), vmem((1024, 256), BF16),
            vmem((2, 1024, 128), F32), vmem((2, 1024, 128), F32), vmem((2, 1024, 128), F32),
            vmem((8, 272, 128), BF16), vmem((8, 272, 128), BF16), vmem((256, 128), F32), vmem((4096, 128), BF16),
            dma((2,)), dma((2,)), dma((2, 2)), dma((8,)), dma(()), dma((8, 2)),
            *[dma((2, 8)) for _ in range(8)], *[dma((8,)) for _ in range(4)],
            *[dma((2,)) for _ in range(2)], *[dma((8, 2)) for _ in range(6)],
        ],
        compiler_params=pltpu.CompilerParams(
            collective_id=0, has_side_effects=True, vmem_limit_bytes=56 * 1024 * 1024),
    )(activations.reshape(br_here * toks, width), out_grads.reshape(br_here * toks, width),
      proj_in, proj_out, fisher_inv, store, lengths, judge_ids.reshape(1, -1))
    return pl.pallas_call(
        widen,
        out_shape=jax.ShapeDtypeStruct((4096, 128), F32),
        in_specs=[any_spec],
        out_specs=any_spec,
        scratch_shapes=[vmem((4096, 128), BF16), vmem((4096, 128), F32), dma((8,)), dma((8,))],
    )(sums)


def solution(mesh):
    placed = (
        P(("grp", "col"), None, "row"),
        P(("grp", "col"), None, "row"),
        P("row", None),
        P("row", None),
        P("row", ("grp", "col")),
        P("row", ("grp", "col")),
        P(("grp", "col")),
        P(),
    )
    return jax.shard_map(
        local, mesh=mesh, in_specs=placed, out_specs=P("row", None), check_vma=False
    )
```

```python
import jax
import jax.numpy as jnp
from jax import lax
from jax.experimental import pallas as pl
from jax.experimental.pallas import tpu as pltpu
from jax.sharding import PartitionSpec as P

MESH = pl.DeviceIdType.MESH
SENDS = (6, 5, 7, 2, 4, 1, 3)
WAITS = (1, 3, 4, 2, 5, 7, 6)
F32 = jnp.float32
BF16 = jnp.bfloat16
SPAN = 80.0


def bound(x):
    top = jnp.max(jnp.abs(x), axis=0, keepdims=True)
    return (top * 1.01 + 1e-36).astype(BF16)


def encode(x, m):
    y = jnp.exp(jnp.abs(x) * (SPAN / m) - 0.5 * SPAN)
    return jnp.where(x < 0, -y, y).astype(BF16)


def decode(y, m):
    y = y.astype(F32)
    t = (jnp.log(jnp.abs(y)) + 0.5 * SPAN) * (m / SPAN)
    return jnp.where(y < 0, -t, t)


def pack(ref, x):
    rows = x.shape[0]
    m = bound(x)
    ref[0:rows, :] = encode(x, m.astype(F32))
    ref[rows:rows + 16, :] = jnp.broadcast_to(m, (16, x.shape[1]))


def unpack(ref):
    rows = ref.shape[0] - 16
    return decode(ref[0:rows, :], ref[rows:rows + 16, :][:1].astype(F32))


def split(x):
    hi = x.astype(BF16)
    return hi, (x - hi.astype(F32)).astype(BF16)


def dot(a, b):
    return jnp.dot(a, b, preferred_element_type=F32)


def loop(lo, hi, body):
    def step(i, _):
        body(i)
        return 0
    lax.fori_loop(lo, hi, step, 0)


def kernel(
    act, og, pin, pout, fish, store, lens_in, ids_in, out,
    lens, ids, actv, ogv, pinv, poutv, fv, fhi, flo, sv,
    proj, p1s, p1r, acc1, p2s, p2r, p3, gf, amat,
    p4s, p4r, acc4, p5, pre, p6s, p6r, xs, p7s, p7r, acc7, ob,
    ldi, ldw, ld1, ldf, lds, ldo,
    p1ss, p1rs, p2ss, p2rs, p3ss, p3rs, f3ss, f3rs, p4ss, p4rs, p5ss, p5rs,
    p6ss, p6rs, p7ss, p7rs, p8ss, p8rs, f8ss, f8rs,
):
    g = lax.axis_index("grp")
    r = lax.axis_index("row")
    col = lax.axis_index("col")
    y, core = lax.div(col, 2), lax.rem(col, 2)
    q = g * 4 + y
    sib = col + 1 - 2 * core
    rx, rz = lax.div(r, 4), lax.rem(r, 4)
    peers = range(1, 8)
    both = range(2)

    def around(hi, lo, k, sign):
        return lax.rem(hi + k // 4, 2) * 4 + lax.rem(lo + (k % 4 if sign > 0 else 4 - k % 4), 4)

    row_to = [around(rx, rz, k, 1) for k in range(8)]
    row_from = [around(rx, rz, k, -1) for k in range(8)]
    chip_to = [around(g, y, k, 1) for k in range(8)]
    chip_from = [around(g, y, k, -1) for k in range(8)]
    to_row = [{"row": i} for i in row_to]
    to_chip = [{"grp": lax.rem(g + k // 4, 2), "col": lax.rem(y + k % 4, 4) * 2 + core} for k in range(8)]
    to_sib = {"col": sib}

    def remote(src, dst, ss, rs, dev):
        return pltpu.make_async_remote_copy(
            src_ref=src, dst_ref=dst, send_sem=ss, recv_sem=rs, device_id=dev, device_id_type=MESH)

    load_w = [pltpu.make_async_copy(pin, pinv, ldw.at[0]), pltpu.make_async_copy(pout, poutv, ldw.at[1])]

    def load_tokens(h, which):
        rows = pl.ds(512 * h, 512)
        src, dst = ((act, actv), (og, ogv))[which]
        return pltpu.make_async_copy(src.at[rows, :], dst.at[rows, :], ld1.at[h, which])

    load_w[0].start()
    load_tokens(0, 0).start()
    load_w[1].start()
    load_tokens(0, 1).start()
    barrier = pltpu.get_barrier_semaphore()
    for k in peers:
        pl.semaphore_signal(barrier, inc=1, device_id=to_row[k], device_id_type=MESH)
        pl.semaphore_signal(barrier, inc=1, device_id=to_chip[k], device_id_type=MESH)
    pl.semaphore_signal(barrier, inc=1, device_id=to_sib, device_id_type=MESH)
    load_tokens(1, 0).start()
    load_tokens(1, 1).start()
    load_lens = pltpu.make_async_copy(lens_in, lens, ldi.at[0])
    load_ids = pltpu.make_async_copy(ids_in, ids, ldi.at[1])
    load_lens.start()
    load_ids.start()

    def f_load(i):
        rows = pl.ds(pl.multiple_of(i * 256, 256), 256)
        return pltpu.make_async_copy(fish.at[rows, :], fv.at[rows, :], ldf.at[i])

    def f_split(i):
        f_load(i).wait()

        def part(j):
            rows = pl.ds(pl.multiple_of(i * 256 + j * 32, 32), 32)
            hi, lo = split(fv[rows, :])
            fhi[rows, :] = hi
            flo[rows, :] = lo
        loop(0, 8, part)

    def p1_copy(h, k):
        return remote(p1s.at[h, k], p1r.at[h, k], p1ss.at[h, k], p1rs.at[h, k], to_row[k])

    for h in both:
        rows = slice(512 * h, 512 * h + 512)
        if h == 0:
            load_w[0].wait()
        load_tokens(h, 0).wait()
        proj[:, 0:128] = dot(actv[rows, :], pinv[...])
        if h == 0:
            load_w[1].wait()
        load_tokens(h, 1).wait()
        proj[:, 128:256] = dot(ogv[rows, :], poutv[...])
        for k in SENDS:
            x = proj[pl.ds(pl.multiple_of(row_to[k] * 64, 64), 64), :]
            m = bound(x)
            code = encode(x, m.astype(F32))
            p1s[h, k, 0:64] = code[:, 0:128]
            p1s[h, k, 64:128] = code[:, 128:256]
            p1s[h, k, 128:144] = jnp.concatenate(
                [jnp.broadcast_to(m[:, 0:128], (8, 128)), jnp.broadcast_to(m[:, 128:256], (8, 128))], axis=0)
            if h == 0 and k == SENDS[0]:
                pl.semaphore_wait(barrier, 15)
            p1_copy(h, k).start()
        acc1[h] = proj[pl.ds(pl.multiple_of(r * 64, 64), 64), :]

    loop(0, 8, lambda i: f_load(i).start())
    load_lens.wait()
    load_ids.wait()
    onehot = (lax.broadcasted_iota(jnp.int32, (128, 256), 0) == ids[...]).astype(F32).astype(BF16)
    place = (lax.broadcasted_iota(jnp.int32, (256, 256), 0), lax.broadcasted_iota(jnp.int32, (256, 256), 1))
    moved = lax.rem(lax.div(place[1], 8), 16) * 16 + lax.div(place[1], 128) * 8 + lax.rem(place[1], 8)
    onehot = dot(onehot, (place[0] == moved).astype(F32).astype(BF16)).astype(BF16)
    loop(0, 5, f_split)

    def p2_copy(h, k):
        rows = pl.ds(pl.multiple_of(row_to[k] * 16, 16), 16)
        return remote(p2s.at[h, rows, :], p2r.at[h, pl.ds(pl.multiple_of(r * 16, 16), 16), :],
                      p2ss.at[h, k], p2rs.at[h, k], to_row[k])

    def p2_arrive(h, k):
        rows = pl.ds(pl.multiple_of(row_from[k] * 16, 16), 16)
        return remote(p2s.at[h, rows, :], p2r.at[h, rows, :], p2ss.at[h, k], p2rs.at[h, k], to_row[k])

    for h in both:
        for k in WAITS:
            p1_copy(h, k).wait_recv()
            m = p1r[h, k, 128:144].astype(F32)
            acc1[h, :, 0:128] += decode(p1r[h, k, 0:64], m[0:1])
            acc1[h, :, 128:256] += decode(p1r[h, k, 64:128], m[8:9])
        total = acc1[h]
        live = lax.broadcasted_iota(jnp.int32, (64, 128), 0) < lens[8 * h + r]
        ahi, alo = split(total[:, 0:128])
        ghi, glo = split(jnp.where(live, total[:, 128:256], 0.0) * 0.125)
        p2s[h] = lax.dot_general(
            jnp.concatenate([ghi, ghi, glo], axis=0), jnp.concatenate([ahi, alo, ahi], axis=0),
            (((0,), (0,)), ((), ())), preferred_element_type=F32)
        for k in SENDS:
            p2_copy(h, k).start()
        own = pl.ds(pl.multiple_of(r * 16, 16), 16)
        p2r[h, own, :] = p2s[h, own, :]
    store_copy = pltpu.make_async_copy(store, sv, lds)
    store_copy.start()
    loop(5, 8, f_split)

    def p3_copy(h, k):
        return remote(p3.at[h, q, core], p3.at[h, q, core], p3ss.at[h, k], p3rs.at[h, k], to_chip[k])

    def p3_arrive(h, k):
        spot = p3.at[h, chip_from[k], core]
        return remote(spot, spot, p3ss.at[h, k], p3rs.at[h, k], to_chip[k])

    def p3_onward(k, which):
        spot = p3.at[1, chip_from[k], which]
        return remote(spot, spot, f3ss.at[1, k], f3rs.at[1, k], to_sib)

    def p3_onward_all(which):
        return remote(p3.at[0, :, which], p3.at[0, :, which], f3ss.at[0, 0], f3rs.at[0, 0], to_sib)

    def use3(h, chip, which):
        x = unpack(p3.at[h, chip, which])
        rows = pl.ds(pl.multiple_of(h * 128 + chip * 16 + which * 8, 8), 8)
        for o in range(16):
            gf[o // 2, rows, (o % 2) * 128:(o % 2) * 128 + 128] = x[8 * o:8 * o + 8]

    for h in both:
        for k in peers:
            p2_arrive(h, k).wait_recv()
        pack(p3.at[h, q, core],
             jnp.concatenate([p2r[h, pl.ds(o, 8, stride=16), :] for o in range(16)], axis=0))
        for k in SENDS:
            p3_copy(h, k).start()
        use3(h, q, core)
    for k in WAITS:
        p3_arrive(0, k).wait_recv()
        use3(0, chip_from[k], core)
    p3_onward_all(core).start()
    p3_onward(0, core).start()
    for k in WAITS:
        p3_arrive(1, k).wait_recv()
        p3_onward(k, core).start()
        use3(1, chip_from[k], core)
    p3_onward_all(1 - core).wait_recv()
    for k in (0, *WAITS):
        use3(0, chip_from[k], 1 - core)
    for k in (0, *WAITS):
        p3_onward(k, 1 - core).wait_recv()
        use3(1, chip_from[k], 1 - core)

    for j in range(8):
        hi, lo = split(gf[j])
        hi, lo = split(dot(onehot, hi) + dot(onehot, lo))
        amat[0:128, 256 * j:256 * j + 256] = hi
        amat[128:256, 256 * j:256 * j + 256] = lo

    def p4_copy(dest):
        return remote(p4s.at[dest], p4r.at[r], p4ss.at[dest], p4rs.at[r], {"row": dest})

    def p4_arrive(k):
        src = row_from[k]
        return remote(p4s.at[src], p4r.at[src], p4ss.at[src], p4rs.at[src], to_row[k])

    def precondition(k):
        p = lax.rem(rx + 1 - lax.rem(k, 2), 2) * 2 + lax.rem(lax.div(rz, 2) + 1 - lax.div(k, 2), 2)
        lanes = pl.ds(pl.multiple_of(p * 256, 256), 256)
        two = dot(amat[...], fhi[:, lanes])
        full = two[0:128] + two[128:256] + dot(amat[0:128, :], flo[:, lanes])
        for e in both:
            dest = 2 * p + e
            part = full[:, e * 128:(e + 1) * 128]
            pack(p4s.at[dest], part)

            @pl.when(dest != r)
            def _():
                p4_copy(dest).start()

            @pl.when(dest == r)
            def _():
                acc4[...] = part
    loop(0, 4, precondition)

    for k in WAITS:
        p4_arrive(k).wait_recv()
        acc4[...] += unpack(p4r.at[row_from[k]])

    def p5_copy(k):
        return remote(p5.at[r], p5.at[r], p5ss.at[k], p5rs.at[k], to_row[k])

    def p5_arrive(k):
        return remote(p5.at[row_from[k]], p5.at[row_from[k]], p5ss.at[k], p5rs.at[k], to_row[k])

    def use5(i, x):
        hi, lo = split(x)
        rows = pl.ds(pl.multiple_of(i * 128, 128), 128)
        pre[rows, 0:128] = hi
        pre[rows, 128:256] = lo

    own5 = acc4[...].T
    pack(p5.at[r], own5)
    for k in (2, 1, 3, 6, 5, 7, 4):
        p5_copy(k).start()
    use5(r, own5)
    store_copy.wait()
    for k in peers:
        for h in both:
            p1_copy(h, k).wait_send()
            p2_copy(h, k).wait_send()
    def score(half, group, part):
        rows = pl.ds(pl.multiple_of(half * 2048 + group * 1024, 1024), 1024)
        feats = pl.ds(pl.multiple_of(part * 512, 512), 512)
        two = dot(sv[rows, feats], pre[feats, :])
        return two[:, 0:128] + two[:, 128:256]

    for k in (1, 3, 2):
        p5_arrive(k).wait_recv()
        use5(row_from[k], unpack(p5.at[row_from[k]]))

    def score_own(u):
        p6s[u] = score(1 - core, u, rx)
        xs[u] = score(core, u, rx)
    loop(0, 2, score_own)
    for k in (4, 5, 7, 6):
        p5_arrive(k).wait_recv()
        use5(row_from[k], unpack(p5.at[row_from[k]]))

    def p6_copy(i, kk):
        spot = (lax.rem(g + 1 + i, 2), pl.ds(pl.multiple_of(lax.rem(y + kk, 4) * 256, 256), 256))
        return remote(p6s.at[spot], p6r.at[spot], p6ss.at[i, kk], p6rs.at[i, kk], to_sib)

    def p6_send(i):
        u = lax.rem(g + 1 + i, 2)
        p6s[u] += score(1 - core, u, 1 - rx)
        for kk in (2, 1, 3, 0):
            p6_copy(i, kk).start()
    loop(0, 2, p6_send)

    parts = (pl.ds(0, 144), pl.ds(144, 128))

    def p7_copy(k, a):
        return remote(p7s.at[k, parts[a]], p7r.at[k, parts[a]], p7ss.at[k, a], p7rs.at[k, a], to_chip[k])

    def p7_first(i):
        u = lax.rem(g + 1 + i, 2)
        xs[u] += score(core, u, 1 - rx)
        for kk in (2, 1, 3, 0):
            p6_copy(i, kk).wait_recv()
            k = 4 - 4 * i + kk
            there = lax.rem(y + kk, 4)
            rows = pl.ds(pl.multiple_of(there * 256, 256), 256)
            x = xs[u, rows, :] + p6r[u, rows, :]
            m = bound(x)
            code = encode(x, m.astype(F32))
            p7s[k, 0:128] = code[0:128]
            p7s[k, 128:144] = jnp.broadcast_to(m, (16, 128))
            p7s[k, 144:272] = code[128:256]
            send = remote(p7s.at[k, parts[0]], p7r.at[k, parts[0]], p7ss.at[k, 0], p7rs.at[k, 0],
                          {"grp": u, "col": there * 2 + core})
            if kk:
                send.start()
            else:
                @pl.when(i == 0)
                def _():
                    send.start()

                @pl.when(i == 1)
                def _():
                    acc7[...] = x
    loop(0, 2, p7_first)
    for k in SENDS:
        p7_copy(k, 1).start()

    for k in peers:
        p4_copy(row_to[k]).wait_send()
        p5_copy(k).wait_send()
        for h in both:
            p3_copy(h, k).wait_send()
    p3_onward_all(core).wait_send()
    for k in range(8):
        p3_onward(k, core).wait_send()

    def p8_copy(k, a):
        rows = pl.ds(128 * a, 128)
        return remote(ob.at[core, q, rows], ob.at[core, q, rows], p8ss.at[k, a], p8rs.at[k, a], to_chip[k])

    def p8_arrive(k, a):
        rows = pl.ds(128 * a, 128)
        spot = ob.at[core, chip_from[k], rows]
        return remote(spot, spot, p8ss.at[k, a], p8rs.at[k, a], to_chip[k])

    def p8_onward(k, which):
        rows = pl.ds(128, 128)
        return remote(ob.at[which, chip_from[k], rows], out.at[which, chip_from[k], rows], f8ss.at[k, 1], f8rs.at[k, 1],
                      to_sib)

    def p8_onward_all(which):
        rows = pl.ds(0, 128)
        return remote(ob.at[which, :, rows], out.at[which, :, rows], f8ss.at[0, 0], f8rs.at[0, 0], to_sib)

    for a in both:
        half = slice(128 * a, 128 * a + 128)
        for k in WAITS:
            p7_copy(k, a).wait_recv()
            acc7[half] += decode(p7r[k, parts[a]][0:128], p7r[k, 128:144][:1].astype(F32))
        ob[core, q, half] = acc7[half].astype(BF16)
        for k in SENDS:
            p8_copy(k, a).start()
    for k in peers:
        for a in both:
            p7_copy(k, a).wait_send()
    for i in both:
        for kk in range(4):
            p6_copy(i, kk).wait_send()
    for k in WAITS:
        p8_arrive(k, 0).wait_recv()
    p8_onward_all(core).start()
    p8_onward(0, core).start()
    for k in peers:
        p8_copy(k, 0).wait_send()
    for k in WAITS:
        p8_arrive(k, 1).wait_recv()
        p8_onward(k, core).start()
    leave = pltpu.make_async_copy(ob.at[core], out.at[core], ldo)
    leave.start()
    for k in peers:
        p8_copy(k, 1).wait_send()
    p8_onward_all(core).wait_send()
    p8_onward_all(1 - core).wait_recv()
    for k in range(8):
        p8_onward(k, core).wait_send()
    for k in range(8):
        p8_onward(k, 1 - core).wait_recv()
    leave.wait()


def widen(src, dst, held, wide, got, put):
    count = got.shape[0]
    rows = src.shape[0] // count

    def load(i):
        part = pl.ds(i * rows, rows)
        return pltpu.make_async_copy(src.at[part, :], held.at[part, :], got.at[i])

    def leave(i):
        part = pl.ds(i * rows, rows)
        return pltpu.make_async_copy(wide.at[part, :], dst.at[part, :], put.at[i])

    for i in range(count):
        load(i).start()
    for i in range(count):
        load(i).wait()
        wide[i * rows:(i + 1) * rows] = held[i * rows:(i + 1) * rows].astype(F32)
        leave(i).start()
    for i in range(count):
        leave(i).wait()


def local(activations, out_grads, proj_in, proj_out, fisher_inv, store, lengths, judge_ids):
    br_here, toks, width = activations.shape
    any_spec = pl.BlockSpec(memory_space=pl.ANY)
    dma = pltpu.SemaphoreType.DMA
    vmem = pltpu.VMEM
    sums = pl.pallas_call(
        kernel,
        out_shape=jax.ShapeDtypeStruct((2, 8, 256, 128), BF16),
        in_specs=[any_spec] * 8,
        out_specs=any_spec,
        scratch_shapes=[
            pltpu.SMEM((16,), jnp.int32), vmem((1, 256), jnp.int32), vmem((1024, 1024), BF16), vmem((1024, 1024), BF16), vmem((1024, 128), BF16), vmem((1024, 128), BF16),
            vmem((2048, 1024), F32), vmem((2048, 1024), BF16), vmem((2048, 1024), BF16), vmem((4096, 1024), BF16),
            vmem((512, 256), F32), vmem((2, 8, 144, 128), BF16), vmem((2, 8, 144, 128), BF16), vmem((2, 64, 256), F32),
            vmem((2, 128, 128), F32), vmem((2, 128, 128), F32), vmem((2, 8, 2, 144, 128), BF16),
            vmem((8, 256, 256), F32), vmem((256, 2048), BF16),
            vmem((8, 144, 128), BF16), vmem((8, 144, 128), BF16), vmem((128, 128), F32),
            vmem((8, 144, 128), BF16), vmem((1024, 256), BF16),
            vmem((2, 1024, 128), F32), vmem((2, 1024, 128), F32), vmem((2, 1024, 128), F32),
            vmem((8, 272, 128), BF16), vmem((8, 272, 128), BF16), vmem((256, 128), F32), vmem((2, 8, 256, 128), BF16),
            dma((2,)), dma((2,)), dma((2, 2)), dma((8,)), dma(()), dma(()),
            *[dma((2, 8)) for _ in range(8)], *[dma((8,)) for _ in range(4)],
            *[dma((2, 4)) for _ in range(2)], *[dma((8, 2)) for _ in range(6)],
        ],
        compiler_params=pltpu.CompilerParams(
            collective_id=0, has_side_effects=True, vmem_limit_bytes=56 * 1024 * 1024),
    )(activations.reshape(br_here * toks, width), out_grads.reshape(br_here * toks, width),
      proj_in, proj_out, fisher_inv, store, lengths, judge_ids.reshape(1, -1))
    return pl.pallas_call(
        widen,
        out_shape=jax.ShapeDtypeStruct((4096, 128), F32),
        in_specs=[any_spec],
        out_specs=any_spec,
        scratch_shapes=[vmem((4096, 128), BF16), vmem((4096, 128), F32), dma((8,)), dma((8,))],
    )(sums.reshape(4096, 128))


def solution(mesh):
    placed = (
        P(("grp", "col"), None, "row"),
        P(("grp", "col"), None, "row"),
        P("row", None),
        P("row", None),
        P("row", ("grp", "col")),
        P("row", ("grp", "col")),
        P(("grp", "col")),
        P(),
    )
    return jax.shard_map(
        local, mesh=mesh, in_specs=placed, out_specs=P("row", None), check_vma=False
    )
```

```python
import jax
import jax.numpy as jnp
from jax import lax
from jax.experimental import pallas as pl
from jax.experimental.pallas import tpu as pltpu
from jax.sharding import PartitionSpec as P

MESH = pl.DeviceIdType.MESH
SENDS = (6, 5, 7, 2, 4, 1, 3)
WAITS = (1, 3, 4, 2, 5, 7, 6)
F32 = jnp.float32
BF16 = jnp.bfloat16
SPAN = 80.0


def bound(x):
    top = jnp.max(jnp.abs(x), axis=0, keepdims=True)
    return (top * 1.01 + 1e-36).astype(BF16)


def encode(x, m):
    y = jnp.exp(jnp.abs(x) * (SPAN / m) - 0.5 * SPAN)
    return jnp.where(x < 0, -y, y).astype(BF16)


def decode(y, m):
    y = y.astype(F32)
    t = (jnp.log(jnp.abs(y)) + 0.5 * SPAN) * (m / SPAN)
    return jnp.where(y < 0, -t, t)


def pack(ref, x):
    rows = x.shape[0]
    m = bound(x)
    ref[0:rows, :] = encode(x, m.astype(F32))
    ref[rows:rows + 16, :] = jnp.broadcast_to(m, (16, x.shape[1]))


def unpack(ref):
    rows = ref.shape[0] - 16
    return decode(ref[0:rows, :], ref[rows:rows + 16, :][:1].astype(F32))


def split(x):
    hi = x.astype(BF16)
    return hi, (x - hi.astype(F32)).astype(BF16)


def dot(a, b):
    return jnp.dot(a, b, preferred_element_type=F32)


def loop(lo, hi, body):
    def step(i, _):
        body(i)
        return 0
    lax.fori_loop(lo, hi, step, 0)


def kernel(
    act, og, pin, pout, fish, store, lens_in, ids_in, out,
    lens, ids, actv, ogv, pinv, poutv, fv, fhi, flo, sv,
    proj, p1s, p1r, acc1, p2s, p2r, p3, gf, amat,
    p4s, p4r, acc4, p5, pre, p6s, p6r, xs, p7s, p7r, acc7, ob,
    ldi, ldw, ld1, ldf, lds, ldo,
    p1ss, p1rs, p2ss, p2rs, p3ss, p3rs, f3ss, f3rs, p4rs, p5rs, p6rs, p7rs, p8rs, f8rs,
):
    g = lax.axis_index("grp")
    r = lax.axis_index("row")
    col = lax.axis_index("col")
    y, core = lax.div(col, 2), lax.rem(col, 2)
    q = g * 4 + y
    sib = col + 1 - 2 * core
    rx, rz = lax.div(r, 4), lax.rem(r, 4)
    peers = range(1, 8)
    both = range(2)

    def around(hi, lo, k, sign):
        return lax.rem(hi + k // 4, 2) * 4 + lax.rem(lo + (k % 4 if sign > 0 else 4 - k % 4), 4)

    row_to = [around(rx, rz, k, 1) for k in range(8)]
    row_from = [around(rx, rz, k, -1) for k in range(8)]
    chip_to = [around(g, y, k, 1) for k in range(8)]
    chip_from = [around(g, y, k, -1) for k in range(8)]
    to_row = [{"row": i} for i in row_to]
    to_chip = [{"grp": lax.rem(g + k // 4, 2), "col": lax.rem(y + k % 4, 4) * 2 + core} for k in range(8)]
    to_sib = {"col": sib}

    def remote(src, dst, ss, rs, dev):
        return pltpu.make_async_remote_copy(
            src_ref=src, dst_ref=dst, send_sem=ss, recv_sem=rs, device_id=dev, device_id_type=MESH)

    load_w = [pltpu.make_async_copy(pin, pinv, ldw.at[0]), pltpu.make_async_copy(pout, poutv, ldw.at[1])]

    def load_tokens(h, which):
        rows = pl.ds(512 * h, 512)
        src, dst = ((act, actv), (og, ogv))[which]
        return pltpu.make_async_copy(src.at[rows, :], dst.at[rows, :], ld1.at[h, which])

    load_w[0].start()
    load_tokens(0, 0).start()
    load_w[1].start()
    load_tokens(0, 1).start()
    barrier = pltpu.get_barrier_semaphore()
    for k in peers:
        pl.semaphore_signal(barrier, inc=1, device_id=to_row[k], device_id_type=MESH)
        pl.semaphore_signal(barrier, inc=1, device_id=to_chip[k], device_id_type=MESH)
    pl.semaphore_signal(barrier, inc=1, device_id=to_sib, device_id_type=MESH)
    load_tokens(1, 0).start()
    load_tokens(1, 1).start()
    load_lens = pltpu.make_async_copy(lens_in, lens, ldi.at[0])
    load_ids = pltpu.make_async_copy(ids_in, ids, ldi.at[1])
    load_lens.start()
    load_ids.start()

    def f_load(i):
        rows = pl.ds(pl.multiple_of(i * 256, 256), 256)
        return pltpu.make_async_copy(fish.at[rows, :], fv.at[rows, :], ldf.at[i])

    def f_split(i):
        f_load(i).wait()

        def part(j):
            rows = pl.ds(pl.multiple_of(i * 256 + j * 32, 32), 32)
            hi, lo = split(fv[rows, :])
            fhi[rows, :] = hi
            flo[rows, :] = lo
        loop(0, 8, part)

    def p1_copy(h, k):
        return remote(p1s.at[h, k], p1r.at[h, k], p1ss.at[h, k], p1rs.at[h, k], to_row[k])

    for h in both:
        rows = slice(512 * h, 512 * h + 512)
        if h == 0:
            load_w[0].wait()
        load_tokens(h, 0).wait()
        proj[:, 0:128] = dot(actv[rows, :], pinv[...])
        if h == 0:
            load_w[1].wait()
        load_tokens(h, 1).wait()
        proj[:, 128:256] = dot(ogv[rows, :], poutv[...])
        for k in SENDS:
            x = proj[pl.ds(pl.multiple_of(row_to[k] * 64, 64), 64), :]
            m = bound(x)
            code = encode(x, m.astype(F32))
            p1s[h, k, 0:64] = code[:, 0:128]
            p1s[h, k, 64:128] = code[:, 128:256]
            p1s[h, k, 128:144] = jnp.concatenate(
                [jnp.broadcast_to(m[:, 0:128], (8, 128)), jnp.broadcast_to(m[:, 128:256], (8, 128))], axis=0)
            if h == 0 and k == SENDS[0]:
                pl.semaphore_wait(barrier, 15)
            p1_copy(h, k).start()
        acc1[h] = proj[pl.ds(pl.multiple_of(r * 64, 64), 64), :]

    loop(0, 8, lambda i: f_load(i).start())
    load_lens.wait()
    load_ids.wait()
    onehot = (lax.broadcasted_iota(jnp.int32, (128, 256), 0) == ids[...]).astype(F32).astype(BF16)
    place = (lax.broadcasted_iota(jnp.int32, (256, 256), 0), lax.broadcasted_iota(jnp.int32, (256, 256), 1))
    moved = lax.rem(lax.div(place[1], 8), 16) * 16 + lax.div(place[1], 128) * 8 + lax.rem(place[1], 8)
    onehot = dot(onehot, (place[0] == moved).astype(F32).astype(BF16)).astype(BF16)
    loop(0, 5, f_split)

    def p2_copy(h, k):
        rows = pl.ds(pl.multiple_of(row_to[k] * 16, 16), 16)
        return remote(p2s.at[h, rows, :], p2r.at[h, pl.ds(pl.multiple_of(r * 16, 16), 16), :],
                      p2ss.at[h, k], p2rs.at[h, k], to_row[k])

    def p2_arrive(h, k):
        rows = pl.ds(pl.multiple_of(row_from[k] * 16, 16), 16)
        return remote(p2s.at[h, rows, :], p2r.at[h, rows, :], p2ss.at[h, k], p2rs.at[h, k], to_row[k])

    for h in both:
        for k in WAITS:
            p1_copy(h, k).wait_recv()
            m = p1r[h, k, 128:144].astype(F32)
            acc1[h, :, 0:128] += decode(p1r[h, k, 0:64], m[0:1])
            acc1[h, :, 128:256] += decode(p1r[h, k, 64:128], m[8:9])
        total = acc1[h]
        live = lax.broadcasted_iota(jnp.int32, (64, 128), 0) < lens[8 * h + r]
        ahi, alo = split(total[:, 0:128])
        ghi, glo = split(jnp.where(live, total[:, 128:256], 0.0) * 0.125)
        p2s[h] = lax.dot_general(
            jnp.concatenate([ghi, ghi, glo], axis=0), jnp.concatenate([ahi, alo, ahi], axis=0),
            (((0,), (0,)), ((), ())), preferred_element_type=F32)
        for k in SENDS:
            p2_copy(h, k).start()
        own = pl.ds(pl.multiple_of(r * 16, 16), 16)
        p2r[h, own, :] = p2s[h, own, :]
    store_copy = pltpu.make_async_copy(store, sv, lds)
    store_copy.start()
    loop(5, 8, f_split)

    def p3_copy(h, k):
        return remote(p3.at[h, q, core], p3.at[h, q, core], p3ss.at[h, k], p3rs.at[h, k], to_chip[k])

    def p3_arrive(h, k):
        spot = p3.at[h, chip_from[k], core]
        return remote(spot, spot, p3ss.at[h, k], p3rs.at[h, k], to_chip[k])

    def p3_onward(k, which):
        spot = p3.at[1, chip_from[k], which]
        return remote(spot, spot, f3ss.at[1, k], f3rs.at[1, k], to_sib)

    def p3_onward_all(which):
        return remote(p3.at[0, :, which], p3.at[0, :, which], f3ss.at[0, 0], f3rs.at[0, 0], to_sib)

    def use3(h, chip, which):
        x = unpack(p3.at[h, chip, which])
        rows = pl.ds(pl.multiple_of(h * 128 + chip * 16 + which * 8, 8), 8)
        for o in range(16):
            gf[o // 2, rows, (o % 2) * 128:(o % 2) * 128 + 128] = x[8 * o:8 * o + 8]

    for h in both:
        for k in peers:
            p2_arrive(h, k).wait_recv()
        pack(p3.at[h, q, core],
             jnp.concatenate([p2r[h, pl.ds(o, 8, stride=16), :] for o in range(16)], axis=0))
        for k in SENDS:
            p3_copy(h, k).start()
        use3(h, q, core)
    for k in peers:
        for h in both:
            p1_copy(h, k).wait_send()
            p2_copy(h, k).wait_send()
    for k in WAITS:
        p3_arrive(0, k).wait_recv()
        use3(0, chip_from[k], core)
    p3_onward_all(core).start()
    p3_onward(0, core).start()
    for k in WAITS:
        p3_arrive(1, k).wait_recv()
        p3_onward(k, core).start()
        use3(1, chip_from[k], core)
    p3_onward_all(1 - core).wait_recv()
    for k in (0, *WAITS):
        use3(0, chip_from[k], 1 - core)
    for k in (0, *WAITS):
        p3_onward(k, 1 - core).wait_recv()
        use3(1, chip_from[k], 1 - core)

    for j in range(8):
        hi, lo = split(gf[j])
        hi, lo = split(dot(onehot, hi) + dot(onehot, lo))
        amat[0:128, 256 * j:256 * j + 256] = hi
        amat[128:256, 256 * j:256 * j + 256] = lo

    def p4_copy(dest):
        return remote(p4s.at[dest], p4r.at[r], p1ss.at[0, dest], p4rs.at[r], {"row": dest})

    def p4_arrive(k):
        src = row_from[k]
        return remote(p4s.at[src], p4r.at[src], p1ss.at[0, src], p4rs.at[src], to_row[k])

    def precondition(k):
        p = lax.rem(rx + 1 - lax.rem(k, 2), 2) * 2 + lax.rem(lax.div(rz, 2) + 1 - lax.div(k, 2), 2)
        lanes = pl.ds(pl.multiple_of(p * 256, 256), 256)
        two = dot(amat[...], fhi[:, lanes])
        full = two[0:128] + two[128:256] + dot(amat[0:128, :], flo[:, lanes])
        for e in both:
            dest = 2 * p + e
            part = full[:, e * 128:(e + 1) * 128]
            pack(p4s.at[dest], part)

            @pl.when(dest != r)
            def _():
                p4_copy(dest).start()

            @pl.when(dest == r)
            def _():
                acc4[...] = part
    loop(0, 4, precondition)

    for k in WAITS:
        p4_arrive(k).wait_recv()
        acc4[...] += unpack(p4r.at[row_from[k]])

    def p5_copy(k):
        return remote(p5.at[r], p5.at[r], p1ss.at[1, k], p5rs.at[k], to_row[k])

    def p5_arrive(k):
        return remote(p5.at[row_from[k]], p5.at[row_from[k]], p1ss.at[1, k], p5rs.at[k], to_row[k])

    def use5(i, x):
        hi, lo = split(x)
        rows = pl.ds(pl.multiple_of(i * 128, 128), 128)
        pre[rows, 0:128] = hi
        pre[rows, 128:256] = lo

    own5 = acc4[...].T
    pack(p5.at[r], own5)
    for k in (2, 1, 3, 6, 5, 7, 4):
        p5_copy(k).start()
    use5(r, own5)
    store_copy.wait()
    for k in peers:
        for h in both:
            p3_copy(h, k).wait_send()
    p3_onward_all(core).wait_send()
    for k in range(8):
        p3_onward(k, core).wait_send()
    def score(half, group, part):
        rows = pl.ds(pl.multiple_of(half * 2048 + group * 1024, 1024), 1024)
        feats = pl.ds(pl.multiple_of(part * 512, 512), 512)
        two = dot(sv[rows, feats], pre[feats, :])
        return two[:, 0:128] + two[:, 128:256]

    for k in (1, 3, 2):
        p5_arrive(k).wait_recv()
        use5(row_from[k], unpack(p5.at[row_from[k]]))

    def score_own(u):
        p6s[u] = score(1 - core, u, rx)
        xs[u] = score(core, u, rx)
    loop(0, 2, score_own)
    for k in (4, 5, 7, 6):
        p5_arrive(k).wait_recv()
        use5(row_from[k], unpack(p5.at[row_from[k]]))

    def p6_copy(i, kk):
        spot = (lax.rem(g + 1 + i, 2), pl.ds(pl.multiple_of(lax.rem(y + kk, 4) * 256, 256), 256))
        return remote(p6s.at[spot], p6r.at[spot], p2ss.at[0, i * 4 + kk], p6rs.at[i, kk], to_sib)

    def p6_send(i):
        u = lax.rem(g + 1 + i, 2)
        p6s[u] += score(1 - core, u, 1 - rx)
        for kk in (2, 1, 3, 0):
            p6_copy(i, kk).start()
    loop(0, 2, p6_send)

    parts = (pl.ds(0, 144), pl.ds(144, 128))

    def p7_copy(k, a):
        return remote(p7s.at[k, parts[a]], p7r.at[k, parts[a]], (p2ss, p3ss)[a].at[1, k], p7rs.at[k, a], to_chip[k])

    def p7_first(i):
        u = lax.rem(g + 1 + i, 2)
        xs[u] += score(core, u, 1 - rx)
        for kk in (2, 1, 3, 0):
            p6_copy(i, kk).wait_recv()
            k = 4 - 4 * i + kk
            there = lax.rem(y + kk, 4)
            rows = pl.ds(pl.multiple_of(there * 256, 256), 256)
            x = xs[u, rows, :] + p6r[u, rows, :]
            m = bound(x)
            code = encode(x, m.astype(F32))
            p7s[k, 0:128] = code[0:128]
            p7s[k, 128:144] = jnp.broadcast_to(m, (16, 128))
            p7s[k, 144:272] = code[128:256]
            send = remote(p7s.at[k, parts[0]], p7r.at[k, parts[0]], p2ss.at[1, k], p7rs.at[k, 0],
                          {"grp": u, "col": there * 2 + core})
            if kk:
                send.start()
            else:
                @pl.when(i == 0)
                def _():
                    send.start()

                @pl.when(i == 1)
                def _():
                    acc7[...] = x
    loop(0, 2, p7_first)
    for k in SENDS:
        p7_copy(k, 1).start()

    for k in peers:
        p4_copy(row_to[k]).wait_send()
        p5_copy(k).wait_send()

    def p8_copy(k, a):
        rows = pl.ds(128 * a, 128)
        return remote(ob.at[core, q, rows], ob.at[core, q, rows], (p3ss, p1ss)[a].at[0, k], p8rs.at[k, a], to_chip[k])

    def p8_arrive(k, a):
        rows = pl.ds(128 * a, 128)
        spot = ob.at[core, chip_from[k], rows]
        return remote(spot, spot, (p3ss, p1ss)[a].at[0, k], p8rs.at[k, a], to_chip[k])

    def p8_onward(k, which):
        rows = pl.ds(128, 128)
        return remote(ob.at[which, chip_from[k], rows], out.at[which, chip_from[k], rows], f3ss.at[1, k], f8rs.at[k, 1],
                      to_sib)

    def p8_onward_all(which):
        rows = pl.ds(0, 128)
        return remote(ob.at[which, :, rows], out.at[which, :, rows], f3ss.at[0, 0], f8rs.at[0, 0], to_sib)

    for a in both:
        half = slice(128 * a, 128 * a + 128)
        for k in WAITS:
            p7_copy(k, a).wait_recv()
            acc7[half] += decode(p7r[k, parts[a]][0:128], p7r[k, 128:144][:1].astype(F32))
        ob[core, q, half] = acc7[half].astype(BF16)
        for k in SENDS:
            p8_copy(k, a).start()
    for k in peers:
        for a in both:
            p7_copy(k, a).wait_send()
    for i in both:
        for kk in range(4):
            p6_copy(i, kk).wait_send()
    for k in WAITS:
        p8_arrive(k, 0).wait_recv()
    p8_onward_all(core).start()
    p8_onward(0, core).start()
    for k in peers:
        p8_copy(k, 0).wait_send()
    for k in WAITS:
        p8_arrive(k, 1).wait_recv()
        p8_onward(k, core).start()
    leave = pltpu.make_async_copy(ob.at[core], out.at[core], ldo)
    leave.start()
    for k in peers:
        p8_copy(k, 1).wait_send()
    p8_onward_all(core).wait_send()
    p8_onward_all(1 - core).wait_recv()
    for k in range(8):
        p8_onward(k, core).wait_send()
    for k in range(8):
        p8_onward(k, 1 - core).wait_recv()
    leave.wait()


def widen(src, dst, held, wide, got, put):
    count = got.shape[0]
    rows = src.shape[0] // count

    def load(i):
        part = pl.ds(i * rows, rows)
        return pltpu.make_async_copy(src.at[part, :], held.at[part, :], got.at[i])

    def leave(i):
        part = pl.ds(i * rows, rows)
        return pltpu.make_async_copy(wide.at[part, :], dst.at[part, :], put.at[i])

    for i in range(count):
        load(i).start()
    for i in range(count):
        load(i).wait()
        wide[i * rows:(i + 1) * rows] = held[i * rows:(i + 1) * rows].astype(F32)
        leave(i).start()
    for i in range(count):
        leave(i).wait()


def local(activations, out_grads, proj_in, proj_out, fisher_inv, store, lengths, judge_ids):
    br_here, toks, width = activations.shape
    any_spec = pl.BlockSpec(memory_space=pl.ANY)
    dma = pltpu.SemaphoreType.DMA
    vmem = pltpu.VMEM
    sums = pl.pallas_call(
        kernel,
        out_shape=jax.ShapeDtypeStruct((2, 8, 256, 128), BF16),
        in_specs=[any_spec] * 8,
        out_specs=any_spec,
        scratch_shapes=[
            pltpu.SMEM((16,), jnp.int32), vmem((1, 256), jnp.int32), vmem((1024, 1024), BF16), vmem((1024, 1024), BF16), vmem((1024, 128), BF16), vmem((1024, 128), BF16),
            vmem((2048, 1024), F32), vmem((2048, 1024), BF16), vmem((2048, 1024), BF16), vmem((4096, 1024), BF16),
            vmem((512, 256), F32), vmem((2, 8, 144, 128), BF16), vmem((2, 8, 144, 128), BF16), vmem((2, 64, 256), F32),
            vmem((2, 128, 128), F32), vmem((2, 128, 128), F32), vmem((2, 8, 2, 144, 128), BF16),
            vmem((8, 256, 256), F32), vmem((256, 2048), BF16),
            vmem((8, 144, 128), BF16), vmem((8, 144, 128), BF16), vmem((128, 128), F32),
            vmem((8, 144, 128), BF16), vmem((1024, 256), BF16),
            vmem((2, 1024, 128), F32), vmem((2, 1024, 128), F32), vmem((2, 1024, 128), F32),
            vmem((8, 272, 128), BF16), vmem((8, 272, 128), BF16), vmem((256, 128), F32), vmem((2, 8, 256, 128), BF16),
            dma((2,)), dma((2,)), dma((2, 2)), dma((8,)), dma(()), dma(()),
            *[dma((2, 8)) for _ in range(8)], dma((8,)), dma((8,)), dma((2, 4)), *[dma((8, 2)) for _ in range(3)],
        ],
        compiler_params=pltpu.CompilerParams(
            collective_id=0, has_side_effects=True, vmem_limit_bytes=56 * 1024 * 1024),
    )(activations.reshape(br_here * toks, width), out_grads.reshape(br_here * toks, width),
      proj_in, proj_out, fisher_inv, store, lengths, judge_ids.reshape(1, -1))
    return pl.pallas_call(
        widen,
        out_shape=jax.ShapeDtypeStruct((4096, 128), F32),
        in_specs=[any_spec],
        out_specs=any_spec,
        scratch_shapes=[vmem((4096, 128), BF16), vmem((4096, 128), F32), dma((8,)), dma((8,))],
    )(sums.reshape(4096, 128))


def solution(mesh):
    placed = (
        P(("grp", "col"), None, "row"),
        P(("grp", "col"), None, "row"),
        P("row", None),
        P("row", None),
        P("row", ("grp", "col")),
        P("row", ("grp", "col")),
        P(("grp", "col")),
        P(),
    )
    return jax.shard_map(
        local, mesh=mesh, in_specs=placed, out_specs=P("row", None), check_vma=False
    )
```
